256 devices in a mesh: section: 8 (over y, x_hi), dp: 32 (over z, x_lo, core).
Axes of the slice: x: 4 (x_hi: 2, x_lo: 2; x = x_hi * 2 + x_lo), y: 4, z: 8, core: 2. Of those that a mesh axis runs over, the one named last changes fastest.
Arguments:
- clips: bfloat16 [64, 14, 8, 640], P('dp'), may hold values from -6 to 6
- cotangent: bfloat16 [64, 14, 8, 640], P('dp'), may hold values from -6 to 6
- timesteps: int32 [64], P('dp'), may hold values from 0 to 999
- time_table: bfloat16 [8, 1000, 640], P('section'), may hold values from -3 to 3
- skip_weights: bfloat16 [8, 640, 640], P('section'), may hold values from -0.125 to 0.125
- conv_weights: bfloat16 [8, 1920, 640], P('section'), may hold values from -0.125 to 0.125
- gains: float32 [8, 640], P('section'), may hold values from 0.5 to 1.5
Outputs:
- grad_skip: float32 [8, 640, 640], P('section')
- grad_conv: float32 [8, 1920, 640], P('section')
- grad_gain: float32 [8, 640], P('section')
The draws below stay inside these ranges and needn't reach their ends.
All inputs are finite; a program needn't handle non-finite values.
Results may differ from the reference program's by a relative error of at most 0.017.
Values may be sent and summed in bfloat16 or wider, within the bound.
No kernel may reach another device: no remote copies, remote signals or barrier semaphores. Data moves between devices by JAX's collectives and lax.ppermute only.
A program may use at most 64 MiB of HBM per device.

```python
import jax
import jax.numpy as jnp
from jax import lax

C = 640
FRAMES = 14
PIXELS = 8
STEPS = 1000
LEVELS = 8
CLIPS = 64


def plant(entries, stream_key, least, high):
    spot = [jax.random.randint(jax.random.fold_in(stream_key, axis), (), 0, length) for axis, length in enumerate(entries.shape)]
    widest = entries.shape.index(max(entries.shape))
    neighbour = spot[:widest] + [(spot[widest] + 1) % entries.shape[widest]] + spot[widest + 1:]
    return entries.at[tuple(spot)].set(least).at[tuple(neighbour)].set(high)


def steps_of(own_key, dims, shards, smallest, largest):
    level = 1.0
    for position, shards_of in shards:
        heights = jax.random.uniform(jax.random.fold_in(jax.random.fold_in(own_key, 6), position), (shards_of,), jnp.float32, smallest / len(shards), largest / len(shards))
        level = level * jnp.repeat(jnp.exp(heights), dims[position] // shards_of).reshape((-1,) + (1,) * (len(dims) - 1 - position))
    return level


def bell_draw(own_key, extent, spread, most, pieces=(), dtype=jnp.bfloat16):
    values = spread * jax.random.normal(own_key, extent, jnp.float32)
    if pieces:
        values = values * steps_of(own_key, extent, pieces, -0.22, 0.18)
    return jnp.clip(values, -most, most).astype(dtype)


def setup_inputs(seed: int = 0) -> dict:
    keys = jax.random.split(jax.random.key(seed), 8)
    clips = bell_draw(keys[0], (CLIPS, FRAMES, PIXELS, C), 1.0, 6.0, ((0, 32),))
    cotangent = bell_draw(keys[1], (CLIPS, FRAMES, PIXELS, C), 1.0, 6.0, ((0, 32),))
    timesteps = plant(jax.random.randint(keys[2], (CLIPS,), 0, STEPS), jax.random.fold_in(keys[2], 1), 0, STEPS - 1).astype(jnp.int32)
    time_table = bell_draw(keys[3], (LEVELS, STEPS, C), 0.5, 3.0, ((0, 8),))
    skip_weights = bell_draw(keys[4], (LEVELS, C, C), (4 * C) ** -0.5, 0.125, ((0, 8),))
    conv_weights = bell_draw(keys[5], (LEVELS, 3 * C, C), (3 * C) ** -0.5, 0.125, ((0, 8),))
    gains = jnp.clip(1.0 + 0.1 * jax.random.normal(keys[6], (LEVELS, C), jnp.float32), 0.5, 1.5)
    return dict(clips=clips, cotangent=cotangent, timesteps=timesteps, time_table=time_table, skip_weights=skip_weights, conv_weights=conv_weights, gains=gains)


EPSILON = 1e-05

def stack_taps(normed):
    zero_frame = jnp.zeros_like(normed[..., :1, :, :])
    before = jnp.concatenate([zero_frame, normed[..., :-1, :, :]], axis=-3)
    after = jnp.concatenate([normed[..., 1:, :, :], zero_frame], axis=-3)
    return jnp.concatenate([before, normed, after], axis=-1)

def unstack_taps(tapped):
    width = tapped.shape[-1] // 3
    first_tap = tapped[..., :width]
    middle_tap = tapped[..., width:2 * width]
    last_tap = tapped[..., 2 * width:]
    zero_frame = jnp.zeros_like(first_tap[..., :1, :, :])
    later = jnp.concatenate([first_tap[..., 1:, :, :], zero_frame], axis=-3)
    earlier = jnp.concatenate([zero_frame, last_tap[..., :-1, :, :]], axis=-3)
    return middle_tap + later + earlier

def flat_dot(left, right):
    rows = left.reshape(-1, left.shape[-1])
    result = jnp.dot(rows, right, preferred_element_type=jnp.float32)
    return result.reshape(left.shape[:-1] + (right.shape[-1],))

def outer_sum(left, right):
    rows_left = left.reshape(-1, left.shape[-1])
    rows_right = right.reshape(-1, right.shape[-1])
    return jnp.dot(rows_left.T, rows_right, preferred_element_type=jnp.float32)

def forward_level(inbound, skip_in, skip_weight, conv_weight, gain_row, embed):
    mixed = inbound.astype(jnp.float32) + flat_dot(skip_in, skip_weight) + embed
    inv_rms = lax.rsqrt(lax.optimization_barrier(jnp.mean(mixed * mixed, axis=-1, keepdims=True)) + EPSILON)
    normed = (mixed * inv_rms * gain_row).astype(jnp.bfloat16)
    conv_out = flat_dot(stack_taps(normed), conv_weight)
    output = (mixed + jax.nn.silu(conv_out)).astype(jnp.bfloat16)
    return (output, mixed, normed, conv_out)

def backward_level(upstream, skip_in, mixed, normed, conv_out, skip_weight, conv_weight, gain_row):
    inv_rms = lax.rsqrt(lax.optimization_barrier(jnp.mean(mixed * mixed, axis=-1, keepdims=True)) + EPSILON)
    sigmoid = jax.nn.sigmoid(conv_out)
    conv_grad = (upstream * sigmoid * (1.0 + conv_out * (1.0 - sigmoid))).astype(jnp.bfloat16)
    grad_conv = outer_sum(stack_taps(normed), conv_grad)
    normed_grad = unstack_taps(flat_dot(conv_grad, conv_weight.T))
    unit = mixed * inv_rms
    grad_gain = lax.optimization_barrier(jnp.sum((normed_grad * unit).reshape(-1, unit.shape[-1]), axis=0))
    scaled = normed_grad * gain_row
    mixed_grad = upstream + inv_rms * (scaled - unit * lax.optimization_barrier(jnp.mean(scaled * unit, axis=-1, keepdims=True)))
    mixed_low = mixed_grad.astype(jnp.bfloat16)
    grad_skip = outer_sum(skip_in, mixed_low)
    skip_grad = flat_dot(mixed_low, skip_weight.T)
    return (mixed_grad, skip_grad, grad_skip, grad_conv, grad_gain)

def reference(clips, cotangent, timesteps, time_table, skip_weights, conv_weights, gains):
    half_levels = LEVELS // 2
    outputs = []
    saved = []
    inbound = clips
    for level_index in range(LEVELS):
        if level_index < half_levels:
            skip_in = inbound
        else:
            skip_in = outputs[LEVELS - 1 - level_index]
        embed = time_table[level_index][timesteps].astype(jnp.float32)[:, None, None, :]
        output, mixed, normed, conv_out = forward_level(inbound, skip_in, skip_weights[level_index], conv_weights[level_index], gains[level_index], embed)
        saved.append((skip_in, mixed, normed, conv_out))
        outputs.append(output)
        inbound = output
    skip_grads = [None] * LEVELS
    grads_skip = [None] * LEVELS
    grads_conv = [None] * LEVELS
    grads_gain = [None] * LEVELS
    passed = cotangent
    for level_index in reversed(range(LEVELS)):
        upstream = passed.astype(jnp.float32)
        if level_index < half_levels:
            upstream = upstream + skip_grads[LEVELS - 1 - level_index].astype(jnp.float32)
        skip_in, mixed, normed, conv_out = saved[level_index]
        mixed_grad, skip_grad, grad_skip, grad_conv, grad_gain = backward_level(upstream, skip_in, mixed, normed, conv_out, skip_weights[level_index], conv_weights[level_index], gains[level_index])
        if level_index < half_levels:
            passed = (mixed_grad + skip_grad).astype(jnp.bfloat16)
        else:
            passed = mixed_grad.astype(jnp.bfloat16)
            skip_grads[level_index] = skip_grad.astype(jnp.bfloat16)
        grads_skip[level_index] = grad_skip / CLIPS
        grads_conv[level_index] = grad_conv / CLIPS
        grads_gain[level_index] = grad_gain / CLIPS
    return (jnp.stack(grads_skip), jnp.stack(grads_conv), jnp.stack(grads_gain))
```

```python
import jax
import jax.numpy as jnp
from jax import lax
from jax.experimental import pallas as pl
from jax.experimental.pallas import tpu as pltpu
from jax.sharding import PartitionSpec as P

EPSILON = 1e-05
LOW = jnp.bfloat16
HIGH = jnp.float32
VMEM_BYTES = 24 * 2**20


def dot(left, right):
    return lax.dot_general(left, right, (((1,), (0,)), ((), ())), preferred_element_type=HIGH)


def dot_transposed(left, right):
    return lax.dot_general(left, right, (((1,), (1,)), ((), ())), preferred_element_type=HIGH)


def dot_outer(left, right):
    return lax.dot_general(left, right, (((0,), (0,)), ((), ())), preferred_element_type=HIGH)


def later(value, pixels):
    return jnp.concatenate([jnp.zeros_like(value[:pixels]), value[:-pixels]], axis=0)


def earlier(value, pixels):
    return jnp.concatenate([value[pixels:], jnp.zeros_like(value[:pixels])], axis=0)


def level_forward(x, s, skip_ref, conv_ref, gain, embed, pixels):
    width = skip_ref.shape[0]
    mixed = x.astype(HIGH) + dot(s, skip_ref[...]) + embed
    inv_rms = lax.rsqrt(jnp.mean(mixed * mixed, axis=-1, keepdims=True) + EPSILON)
    unit = mixed * inv_rms
    normed = (unit * gain).astype(LOW)
    before = dot(normed, conv_ref[:width])
    middle = dot(normed, conv_ref[width : 2 * width])
    after = dot(normed, conv_ref[2 * width :])
    conv_out = middle + later(before, pixels) + earlier(after, pixels)
    return mixed, inv_rms, unit, normed, conv_out


def forward_kernel(pixels, same, *refs):
    if same:
        x_ref, skip_ref, conv_ref, gain_ref, embed_ref, out_ref = refs
        x = x_ref[...]
        s = x
    else:
        x_ref, s_ref, skip_ref, conv_ref, gain_ref, embed_ref, out_ref = refs
        x = x_ref[...]
        s = s_ref[...]
    mixed, _, _, _, conv_out = level_forward(
        x, s, skip_ref, conv_ref, gain_ref[...], embed_ref[...], pixels
    )
    out_ref[...] = (mixed + conv_out * jax.nn.sigmoid(conv_out)).astype(LOW)


def saved_kernel(pixels, x_ref, s_ref, skip_ref, conv_ref, gain_ref, embed_ref,
                 inv_ref, unit_ref, normed_ref, slope_ref):
    _, inv_rms, unit, normed, conv_out = level_forward(
        x_ref[...], s_ref[...], skip_ref, conv_ref, gain_ref[...], embed_ref[...], pixels
    )
    sigmoid = jax.nn.sigmoid(conv_out)
    inv_ref[...] = jnp.broadcast_to(inv_rms, inv_ref.shape)
    unit_ref[...] = unit
    normed_ref[...] = normed
    slope_ref[...] = sigmoid * (1.0 + conv_out * (1.0 - sigmoid))


def level_backward(d, slope, unit, inv_rms, conv_ref, gain, pixels):
    width = conv_ref.shape[1]
    conv_grad = d * slope
    conv_low = conv_grad.astype(LOW)
    first = dot_transposed(conv_low, conv_ref[:width])
    middle = dot_transposed(conv_low, conv_ref[width : 2 * width])
    last = dot_transposed(conv_low, conv_ref[2 * width :])
    normed_grad = middle + earlier(first, pixels) + later(last, pixels)
    scaled = normed_grad * gain
    mixed_grad = d + inv_rms * (
        scaled - unit * jnp.mean(scaled * unit, axis=-1, keepdims=True)
    )
    return conv_grad, normed_grad, mixed_grad


def backward_kernel(pixels, joined, with_skip, *refs):
    if with_skip:
        d_ref, extra_ref, *refs = refs
        d = d_ref[...].astype(HIGH) + extra_ref[...].astype(HIGH)
    else:
        d_ref, *refs = refs
        d = d_ref[...].astype(HIGH)
    inv_ref, unit_ref, slope_ref, skip_ref, conv_ref, gain_ref, *outs = refs
    _, _, mixed_grad = level_backward(
        d, slope_ref[...], unit_ref[...], inv_ref[:, :1], conv_ref, gain_ref[...], pixels
    )
    skip_grad = dot_transposed(mixed_grad.astype(LOW), skip_ref[...])
    if joined:
        outs[0][...] = (mixed_grad + skip_grad).astype(LOW)
    else:
        outs[0][...] = mixed_grad.astype(LOW)
        outs[1][...] = skip_grad.astype(LOW)


def last_kernel(pixels, clips, *refs):
    d_refs, refs = refs[:clips], refs[clips:]
    e_refs, refs = refs[:clips], refs[clips:]
    inv_refs, refs = refs[:clips], refs[clips:]
    unit_refs, refs = refs[:clips], refs[clips:]
    slope_refs, refs = refs[:clips], refs[clips:]
    normed_refs, refs = refs[:clips], refs[clips:]
    s_refs, refs = refs[:clips], refs[clips:]
    conv_ref, gain_ref, grad_ref, gain_out_ref = refs
    width = conv_ref.shape[1]
    gain_total = jnp.zeros((1, width), HIGH)
    shifted = ([], [], [])
    mixed_lows = []
    for c in range(clips):
        d = d_refs[c][...].astype(HIGH) + e_refs[c][...].astype(HIGH)
        unit = unit_refs[c][...]
        conv_grad, normed_grad, mixed_grad = level_backward(
            d, slope_refs[c][...], unit, inv_refs[c][:, :1], conv_ref, gain_ref[...], pixels
        )
        gain_total = gain_total + jnp.sum(normed_grad * unit, axis=0, keepdims=True)
        shifted[0].append(earlier(conv_grad, pixels).astype(LOW))
        shifted[1].append(conv_grad.astype(LOW))
        shifted[2].append(later(conv_grad, pixels).astype(LOW))
        mixed_lows.append(mixed_grad.astype(LOW))
    normed = jnp.concatenate([r[...] for r in normed_refs], axis=0)
    s = jnp.concatenate([r[...] for r in s_refs], axis=0)
    grad_ref[:width] = dot_outer(s, jnp.concatenate(mixed_lows, axis=0)).astype(LOW)
    for tap in range(3):
        grad_ref[(tap + 1) * width : (tap + 2) * width] = dot_outer(
            normed, jnp.concatenate(shifted[tap], axis=0)
        ).astype(LOW)
    gain_out_ref[...] = gain_total


def call(kernel, name, outs, *args):
    single = not isinstance(outs, tuple)
    return pl.pallas_call(
        kernel,
        out_shape=outs,
        name=name,
        compiler_params=pltpu.CompilerParams(vmem_limit_bytes=VMEM_BYTES),
    )(*args)


def make_local(sizes):
    sections = sizes["section"]
    dp = sizes["dp"]
    half = sections // 2
    cross = 2
    ring = dp // 4

    def local(clips, cotangent, timesteps, time_table, skip_weights, conv_weights, gains):
        both = ("section", "dp")
        section = lax.axis_index("section")
        member = lax.axis_index("dp")
        core = member % 2
        z = member // 4
        count, frames, pixels, width = clips.shape
        rows = frames * pixels
        skip_weight = skip_weights[0]
        conv_weight = conv_weights[0]
        gain = gains
        low_rows = jax.ShapeDtypeStruct((rows, width), LOW)
        high_rows = jax.ShapeDtypeStruct((rows, width), HIGH)

        def send(value, source, target):
            flip = cross if (source - target) % 2 else 0
            return lax.ppermute(
                value, both, [(source * dp + i, target * dp + (i ^ flip)) for i in range(dp)]
            )

        def within(value, move, only=range(sections)):
            return lax.ppermute(
                value, both, [(s * dp + i, s * dp + move(i)) for s in only for i in range(dp)]
            )

        odd = section % 2 == 1
        swapped_steps = within(timesteps, lambda i: i ^ cross, range(1, sections, 2))
        steps = jnp.where(odd, swapped_steps, timesteps)
        embeds = jnp.take(time_table[0], steps, axis=0).astype(HIGH)
        embed = [embeds[m : m + 1] for m in range(count)]
        first_clips = [clips[m].reshape(rows, width) for m in range(count)]
        last_cotangent = cotangent.reshape(count, rows, width)
        last_section = sections - 1
        if last_section % 2:
            last_cotangent = within(last_cotangent, lambda i: i ^ cross, [last_section])
        zero = jnp.zeros((rows, width), LOW)

        received = [[None] * sections for _ in range(count)]
        skips = [[None] * sections for _ in range(count)]
        for m in range(count):
            received[m][0] = first_clips[m]
        for t in range(sections - 1):
            for m in range(count):
                x = received[m][t]
                if t <= half:
                    out = call(
                        lambda *r: forward_kernel(pixels, True, *r), "fwd", low_rows,
                        x, skip_weight, conv_weight, gain, embed[m],
                    )
                else:
                    out = call(
                        lambda *r: forward_kernel(pixels, False, *r), "fwd_skip", low_rows,
                        x, skips[m][t], skip_weight, conv_weight, gain, embed[m],
                    )
                received[m][t + 1] = send(out, t, t + 1)
                if t < half - 1:
                    out, _ = lax.optimization_barrier((out, received[m][t + 1]))
                    skips[m][last_section - t] = send(out, t, last_section - t)

        is_first = section == 0
        saved = []
        for m in range(count):
            x = jnp.where(is_first, first_clips[m], zero)
            for t in range(1, sections):
                x = x + received[m][t]
            s = jnp.where(section > half, zero, x)
            for t in range(half + 1, sections):
                s = s + skips[m][t]
            inv, unit, normed, slope = call(
                lambda *r: saved_kernel(pixels, *r), "saved",
                (jax.ShapeDtypeStruct((rows, 128), HIGH), high_rows, low_rows, high_rows),
                x, s, skip_weight, conv_weight, gain, embed[m],
            )
            saved.append((inv, unit, normed, slope, s))

        is_last = section == last_section
        grads = [[None] * sections for _ in range(count)]
        extras = [[None] * half for _ in range(count)]
        for m in range(count):
            grads[m][last_section] = last_cotangent[m]
        for t in range(last_section, 0, -1):
            for m in range(count):
                inv, unit, normed, slope, s = saved[m]
                joined = t <= half
                with_skip = t < half - 1
                args = (grads[m][t],) + ((extras[m][t],) if with_skip else ())
                result = call(
                    lambda *r, joined=joined, with_skip=with_skip: backward_kernel(
                        pixels, joined, with_skip, *r
                    ),
                    "bwd",
                    low_rows if joined else (low_rows, low_rows),
                    *args, inv, unit, slope, skip_weight, conv_weight, gain,
                )
                if joined:
                    grads[m][t - 1] = send(result, t, t - 1)
                else:
                    grads[m][t - 1] = send(result[0], t, t - 1)
                    side, _ = lax.optimization_barrier((result[1], grads[m][t - 1]))
                    extras[m][last_section - t] = send(side, t, last_section - t)

        d_parts = []
        e_parts = []
        for m in range(count):
            e = jnp.where(is_last, last_cotangent[m], zero)
            for t in range(sections - 2, 0, -1):
                e = e + grads[m][t]
            for t in range(half - 1):
                e = e + extras[m][t]
            e_parts.append(e)
            d_parts.append(grads[m][0])
        flat = lambda k: [saved[m][k] for m in range(count)]
        taps = 4
        grad, gain_part = call(
            lambda *r: last_kernel(pixels, count, *r), "last",
            (jax.ShapeDtypeStruct((taps * width, width), LOW), jax.ShapeDtypeStruct((1, width), HIGH)),
            *d_parts, *e_parts, *flat(0), *flat(1), *flat(3), *flat(2), *flat(4),
            conv_weight, gain,
        )
        return finish(grad, gain_part, within, member, core, z, width, count * dp)

    def finish(grad, gain_part, within, member, core, z, width, total):
        summed = lax.psum(grad, "dp").astype(HIGH)
        gain_sum = lax.psum(gain_part, "dp")
        return (
            (summed[:width] / total)[None],
            (summed[width:] / total)[None],
            gain_sum / total,
        )

    return local


def solution(mesh):
    placed = (
        P("dp", None, None, None),
        P("dp", None, None, None),
        P("dp"),
        P("section", None, None),
        P("section", None, None),
        P("section", None, None),
        P("section", None),
    )
    return jax.shard_map(
        make_local(dict(mesh.shape)),
        mesh=mesh,
        in_specs=placed,
        out_specs=(P("section", None, None), P("section", None, None), P("section", None)),
        check_vma=False,
    )
```

```python
import jax
import jax.numpy as jnp
from jax import lax
from jax.experimental import pallas as pl
from jax.experimental.pallas import tpu as pltpu
from jax.sharding import PartitionSpec as P

EPSILON = 1e-05
LOW = jnp.bfloat16
HIGH = jnp.float32
VMEM_BYTES = 12 * 2**20
BIG_BYTES = 32 * 2**20


def dot(left, right):
    return lax.dot_general(left, right, (((1,), (0,)), ((), ())), preferred_element_type=HIGH)


def dot_transposed(left, right):
    return lax.dot_general(left, right, (((1,), (1,)), ((), ())), preferred_element_type=HIGH)


def dot_outer(left, right):
    return lax.dot_general(left, right, (((0,), (0,)), ((), ())), preferred_element_type=HIGH)


def later(value, pixels):
    return jnp.concatenate([jnp.zeros_like(value[:pixels]), value[:-pixels]], axis=0)


def earlier(value, pixels):
    return jnp.concatenate([value[pixels:], jnp.zeros_like(value[:pixels])], axis=0)


def level_forward(x, s, skip_ref, conv_ref, gain, embed, pixels):
    width = skip_ref.shape[0]
    mixed = x.astype(HIGH) + dot(s, skip_ref[...]) + embed
    inv_rms = lax.rsqrt(jnp.mean(mixed * mixed, axis=-1, keepdims=True) + EPSILON)
    unit = mixed * inv_rms
    normed = (unit * gain).astype(LOW)
    before = dot(normed, conv_ref[:width])
    middle = dot(normed, conv_ref[width : 2 * width])
    after = dot(normed, conv_ref[2 * width :])
    conv_out = middle + later(before, pixels) + earlier(after, pixels)
    return mixed, inv_rms, unit, normed, conv_out


def forward_kernel(pixels, same, *refs):
    if same:
        x_ref, skip_ref, conv_ref, gain_ref, embed_ref, out_ref = refs
        x = x_ref[...]
        s = x
    else:
        x_ref, s_ref, skip_ref, conv_ref, gain_ref, embed_ref, out_ref = refs
        x = x_ref[...]
        s = s_ref[...]
    mixed, _, _, _, conv_out = level_forward(
        x, s, skip_ref, conv_ref, gain_ref[...], embed_ref[...], pixels
    )
    out_ref[...] = (mixed + conv_out * jax.nn.sigmoid(conv_out)).astype(LOW)


def saved_kernel(pixels, x_ref, s_ref, skip_ref, conv_ref, gain_ref, embed_ref,
                 inv_ref, unit_ref, normed_ref, slope_ref):
    _, inv_rms, unit, normed, conv_out = level_forward(
        x_ref[...], s_ref[...], skip_ref, conv_ref, gain_ref[...], embed_ref[...], pixels
    )
    sigmoid = jax.nn.sigmoid(conv_out)
    inv_ref[...] = jnp.broadcast_to(inv_rms, inv_ref.shape)
    unit_ref[...] = unit
    normed_ref[...] = normed
    slope_ref[...] = sigmoid * (1.0 + conv_out * (1.0 - sigmoid))


def level_backward(d, slope, unit, inv_rms, conv_ref, gain, pixels):
    width = conv_ref.shape[1]
    conv_grad = d * slope
    conv_low = conv_grad.astype(LOW)
    first = dot_transposed(conv_low, conv_ref[:width])
    middle = dot_transposed(conv_low, conv_ref[width : 2 * width])
    last = dot_transposed(conv_low, conv_ref[2 * width :])
    normed_grad = middle + earlier(first, pixels) + later(last, pixels)
    scaled = normed_grad * gain
    mixed_grad = d + inv_rms * (
        scaled - unit * jnp.mean(scaled * unit, axis=-1, keepdims=True)
    )
    return conv_grad, normed_grad, mixed_grad


def backward_kernel(pixels, joined, with_skip, *refs):
    if with_skip:
        d_ref, extra_ref, *refs = refs
        d = d_ref[...].astype(HIGH) + extra_ref[...].astype(HIGH)
    else:
        d_ref, *refs = refs
        d = d_ref[...].astype(HIGH)
    inv_ref, unit_ref, slope_ref, skip_ref, conv_ref, gain_ref, *outs = refs
    _, _, mixed_grad = level_backward(
        d, slope_ref[...], unit_ref[...], inv_ref[:, :1], conv_ref, gain_ref[...], pixels
    )
    skip_grad = dot_transposed(mixed_grad.astype(LOW), skip_ref[...])
    if joined:
        outs[0][...] = (mixed_grad + skip_grad).astype(LOW)
    else:
        outs[0][...] = mixed_grad.astype(LOW)
        outs[1][...] = skip_grad.astype(LOW)


CHUNK_PAD = 8


def last_kernel(pixels, clips, where_ref, *refs):
    d_refs, refs = refs[:clips], refs[clips:]
    e_refs, refs = refs[:clips], refs[clips:]
    inv_refs, refs = refs[:clips], refs[clips:]
    unit_refs, refs = refs[:clips], refs[clips:]
    slope_refs, refs = refs[:clips], refs[clips:]
    normed_refs, refs = refs[:clips], refs[clips:]
    s_refs, refs = refs[:clips], refs[clips:]
    conv_ref, gain_ref, keep_ref, give_ref, grad_ref = refs
    width = conv_ref.shape[1]
    ring, chunk, _ = keep_ref.shape
    used = chunk - CHUNK_PAD
    gain_total = jnp.zeros((1, width), HIGH)
    shifted = ([], [], [])
    mixed_lows = []
    for c in range(clips):
        d = d_refs[c][...].astype(HIGH) + e_refs[c][...].astype(HIGH)
        unit = unit_refs[c][...]
        conv_grad, normed_grad, mixed_grad = level_backward(
            d, slope_refs[c][...], unit, inv_refs[c][:, :1], conv_ref, gain_ref[...], pixels
        )
        gain_total = gain_total + jnp.sum(normed_grad * unit, axis=0, keepdims=True)
        shifted[0].append(earlier(conv_grad, pixels).astype(LOW))
        shifted[1].append(conv_grad.astype(LOW))
        shifted[2].append(later(conv_grad, pixels).astype(LOW))
        mixed_lows.append(mixed_grad.astype(LOW))
    normed = jnp.concatenate([r[...] for r in normed_refs], axis=0)
    s = jnp.concatenate([r[...] for r in s_refs], axis=0)
    pad = jnp.zeros((2 * ring, CHUNK_PAD, width), LOW)
    grad_ref[:, used:, :] = pad
    grad_ref[0, used:, :] = jnp.broadcast_to(gain_total, (CHUNK_PAD, width)).astype(LOW)
    each = width // used

    def put(matrix, value):
        grad_ref[matrix * each : (matrix + 1) * each, :used, :] = value.astype(LOW).reshape(
            each, used, width
        )

    put(0, dot_outer(s, jnp.concatenate(mixed_lows, axis=0)))
    for tap in range(3):
        put(tap + 1, dot_outer(normed, jnp.concatenate(shifted[tap], axis=0)))
    core = where_ref[0]
    z = where_ref[1]
    for k in range(ring):
        target = lax.rem(z + k, ring)
        keep_ref[k] = grad_ref[core * ring + target]
        give_ref[k] = grad_ref[(1 - core) * ring + target]


def finish_kernel(scale, ring, where_ref, *refs):
    own, other, (skip_ref, conv_ref, gain_ref, all_ref) = refs[:ring], refs[ring : 2 * ring], refs[2 * ring :]
    chunk, width = own[0].shape
    used = chunk - CHUNK_PAD
    core = where_ref[0]
    z = where_ref[1]
    for k in range(ring):
        target = lax.rem(z + k, ring)
        all_ref[core * ring + target] = own[k][...]
        all_ref[(1 - core) * ring + target] = other[k][...]
    each = width // used
    for c in range(2 * ring):
        value = all_ref[c, :used, :].astype(HIGH) * scale
        if c < each:
            skip_ref[0, c * used : (c + 1) * used, :] = value
        else:
            conv_ref[0, (c - each) * used : (c - each + 1) * used, :] = value
    gain_ref[...] = all_ref[0, used : used + 1, :].astype(HIGH) * scale


def call(kernel, name, outs, *args, scratch=(), scalars=0, limit=VMEM_BYTES):
    specs = [pl.BlockSpec(memory_space=pltpu.SMEM)] * scalars + [
        pl.BlockSpec(memory_space=pltpu.VMEM)
    ] * (len(args) - scalars)
    return pl.pallas_call(
        kernel,
        out_shape=outs,
        in_specs=specs,
        name=name,
        scratch_shapes=scratch,
        compiler_params=pltpu.CompilerParams(vmem_limit_bytes=limit),
    )(*args)


def after(value, other):
    return lax.optimization_barrier((value, other))[0]


def make_local(sizes):
    sections = sizes["section"]
    dp = sizes["dp"]
    half = sections // 2
    cross = 2
    ring = dp // 4

    def local(clips, cotangent, timesteps, time_table, skip_weights, conv_weights, gains):
        both = ("section", "dp")
        section = lax.axis_index("section")
        member = lax.axis_index("dp")
        core = member % 2
        z = member // 4
        count, frames, pixels, width = clips.shape
        rows = frames * pixels
        skip_weight = skip_weights[0]
        conv_weight = conv_weights[0]
        gain = gains
        low_rows = jax.ShapeDtypeStruct((rows, width), LOW)
        high_rows = jax.ShapeDtypeStruct((rows, width), HIGH)
        last_section = sections - 1

        def hop(value, pairs):
            return lax.ppermute(
                value,
                both,
                [
                    (source * dp + i, target * dp + (i ^ (cross if (source - target) % 2 else 0)))
                    for source, target in pairs
                    for i in range(dp)
                ],
            )

        def within(value, move, only=range(sections)):
            return lax.ppermute(
                value, both, [(s * dp + i, s * dp + move(i)) for s in only for i in range(dp)]
            )

        odd = section % 2 == 1

        def rows_of(steps):
            return jnp.take(time_table[0], steps, axis=0).astype(HIGH)

        swapped_steps = within(timesteps, lambda i: i ^ cross, range(1, sections, 2))
        embeds = (rows_of(timesteps), rows_of(swapped_steps))
        own_embed = jnp.where(odd, embeds[1], embeds[0])
        first_clips = [clips[m].reshape(rows, width) for m in range(count)]
        last_cotangent = cotangent.reshape(count, rows, width)
        if last_section % 2:
            last_cotangent = within(last_cotangent, lambda i: i ^ cross, [last_section])
        zero = jnp.zeros((rows, width), LOW)

        def own_of(values, levels):
            out = values[levels[0]]
            for t in levels[1:]:
                out = jnp.where(section == t, values[t], out)
            return out

        received = [[None] * sections for _ in range(count)]
        outs = [[None] * sections for _ in range(count)]
        for m in range(count):
            received[m][0] = first_clips[m]
        side_pairs = [(t, last_section - t) for t in range(half - 1)]
        skips = [None] * count
        for t in range(sections - 1):
            for m in range(count):
                x = received[m][t]
                embed = embeds[t % 2][m : m + 1]
                if t <= half:
                    out = call(
                        lambda *r: forward_kernel(pixels, True, *r), "fwd", low_rows,
                        x, skip_weight, conv_weight, gain, embed,
                    )
                else:
                    out = call(
                        lambda *r: forward_kernel(pixels, False, *r), "fwd_skip", low_rows,
                        x, skips[m], skip_weight, conv_weight, gain, embed,
                    )
                outs[m][t] = out
                if m:
                    out = after(out, received[m - 1][t + 1])
                received[m][t + 1] = hop(out, [(t, t + 1)])
            if t == half - 1:
                for m in range(count):
                    side = own_of(outs[m], range(half - 1))
                    side = after(side, skips[m - 1] if m else outs[-1][t])
                    skips[m] = hop(side, side_pairs)

        is_first = section == 0
        saved = []
        for m in range(count):
            x = jnp.where(is_first, first_clips[m], zero)
            for t in range(1, sections):
                x = x + received[m][t]
            s = jnp.where(section > half, skips[m], x)
            inv, unit, normed, slope = call(
                lambda *r: saved_kernel(pixels, *r), "saved",
                (jax.ShapeDtypeStruct((rows, 128), HIGH), high_rows, low_rows, high_rows),
                x, s, skip_weight, conv_weight, gain, own_embed[m : m + 1],
            )
            saved.append((inv, unit, normed, slope, s))

        is_last = section == last_section
        grads = [[None] * sections for _ in range(count)]
        sides = [[None] * sections for _ in range(count)]
        extras = [None] * count
        for m in range(count):
            grads[m][last_section] = last_cotangent[m]
        back_pairs = [(target, source) for source, target in side_pairs]
        for t in range(last_section, 0, -1):
            results = []
            for m in range(count):
                inv, unit, normed, slope, s = saved[m]
                joined = t <= half
                with_skip = t < half - 1
                args = (grads[m][t],) + ((extras[m],) if with_skip else ())
                result = call(
                    lambda *r, joined=joined, with_skip=with_skip: backward_kernel(
                        pixels, joined, with_skip, *r
                    ),
                    "bwd",
                    low_rows if joined else (low_rows, low_rows),
                    *args, inv, unit, slope, skip_weight, conv_weight, gain,
                )
                if not joined:
                    result, sides[m][t] = result
                results.append(result)
                if m:
                    result = after(result, grads[m - 1][t - 1])
                grads[m][t - 1] = hop(result, [(t, t - 1)])
            if t == half:
                for m in range(count):
                    side = own_of(sides[m], range(last_section, half, -1))
                    side = after(side, extras[m - 1] if m else results[-1])
                    extras[m] = hop(side, back_pairs)

        d_parts = []
        e_parts = []
        for m in range(count):
            e = jnp.where(is_last, last_cotangent[m], extras[m])
            for t in range(sections - 2, 0, -1):
                e = e + grads[m][t]
            e_parts.append(e)
            d_parts.append(grads[m][0])
        flat = lambda k: [saved[m][k] for m in range(count)]

        taps = 4
        chunk = taps * width // (2 * ring) + CHUNK_PAD
        chunks = jax.ShapeDtypeStruct((ring, chunk, width), LOW)
        where = jnp.stack([core, z]).astype(jnp.int32)
        keep, give = call(
            lambda *r: last_kernel(pixels, count, *r), "last", (chunks, chunks),
            where, *d_parts, *e_parts, *flat(0), *flat(1), *flat(3), *flat(2), *flat(4),
            conv_weight, gain,
            scratch=[pltpu.VMEM((2 * ring, chunk, width), LOW)], scalars=1, limit=BIG_BYTES,
        )
        to_core = lambda i: i ^ 1
        to_x = lambda i: i ^ cross
        down = lambda i: ((i // 4 - 1) % ring) * 4 + i % 4
        up = lambda i: ((i // 4 + 1) % ring) * 4 + i % 4
        got = within(give, to_core)

        def mine(k):
            return keep[k].astype(HIGH) + got[k].astype(HIGH)

        far = ring // 2
        lower = within(mine(far).astype(LOW), down)
        upper = within(mine(far - 1).astype(LOW), up)
        for k in range(1, far):
            lower = within((lower.astype(HIGH) + mine(far + k)).astype(LOW), down)
            if k < far - 1:
                upper = within((upper.astype(HIGH) + mine(far - 1 - k)).astype(LOW), up)
        part = (mine(0) + lower.astype(HIGH) + upper.astype(HIGH)).astype(LOW)
        part = part + within(part, to_x)
        full = [None] * ring
        full[0] = part
        lower = part
        upper = part
        for k in range(1, far + 1):
            lower = within(lower, down)
            full[k] = lower
            if k < far:
                upper = within(upper, up)
                full[ring - k] = upper
        order = [0]
        for k in range(1, far + 1):
            order.append(k)
            if k < far:
                order.append(ring - k)
        other = [None] * ring
        for n, k in enumerate(order):
            value = full[k]
            if n > 1:
                value = after(value, other[order[n - 2]])
            other[k] = within(value, to_core)
        total = count * dp
        return call(
            lambda *r: finish_kernel(1.0 / total, ring, *r), "finish",
            (
                jax.ShapeDtypeStruct((1, width, width), HIGH),
                jax.ShapeDtypeStruct((1, 3 * width, width), HIGH),
                jax.ShapeDtypeStruct((1, width), HIGH),
            ),
            where, *full, *other,
            scratch=[pltpu.VMEM((2 * ring, chunk, width), LOW)], scalars=1, limit=BIG_BYTES,
        )

    return local


def solution(mesh):
    placed = (
        P("dp", None, None, None),
        P("dp", None, None, None),
        P("dp"),
        P("section", None, None),
        P("section", None, None),
        P("section", None, None),
        P("section", None),
    )
    return jax.shard_map(
        make_local(dict(mesh.shape)),
        mesh=mesh,
        in_specs=placed,
        out_specs=(P("section", None, None), P("section", None, None), P("section", None)),
        check_vma=False,
    )
```

```python
import jax
import jax.numpy as jnp
from jax import lax
from jax.experimental import pallas as pl
from jax.experimental.pallas import tpu as pltpu
from jax.sharding import PartitionSpec as P

EPSILON = 1e-05
LOW = jnp.bfloat16
HIGH = jnp.float32
SMALL_BYTES = 12 * 2**20
BIG_BYTES = 32 * 2**20
CHUNK_PAD = 8
GAIN_ROWS = 16
PIECES = 2


def dot(left, right):
    return lax.dot_general(left, right, (((1,), (0,)), ((), ())), preferred_element_type=HIGH)


def dot_transposed(left, right):
    return lax.dot_general(left, right, (((1,), (1,)), ((), ())), preferred_element_type=HIGH)


def dot_outer(left, right):
    return lax.dot_general(left, right, (((0,), (0,)), ((), ())), preferred_element_type=HIGH)


def later(value, pixels):
    return jnp.concatenate([jnp.zeros_like(value[:pixels]), value[:-pixels]], axis=0)


def earlier(value, pixels):
    return jnp.concatenate([value[pixels:], jnp.zeros_like(value[:pixels])], axis=0)


def level_forward(x, s, weight_ref, level, vec_ref, pixels):
    gain = vec_ref[level : level + 1]
    embed = vec_ref[2 + level : 3 + level]
    mixed = x.astype(HIGH) + dot(s, weight_ref[level, 0]) + embed
    inv_rms = lax.rsqrt(jnp.mean(mixed * mixed, axis=-1, keepdims=True) + EPSILON)
    unit = mixed * inv_rms
    normed = (unit * gain).astype(LOW)
    before = dot(normed, weight_ref[level, 1])
    middle = dot(normed, weight_ref[level, 2])
    after_tap = dot(normed, weight_ref[level, 3])
    conv_out = middle + later(before, pixels) + earlier(after_tap, pixels)
    sigmoid = jax.nn.sigmoid(conv_out)
    out = (mixed + conv_out * sigmoid).astype(LOW)
    return out, inv_rms, unit, normed, sigmoid * (1.0 + conv_out * (1.0 - sigmoid))


def encoder_kernel(pixels, x_ref, weight_ref, vec_ref, first_ref, second_ref):
    x = x_ref[...]
    first = level_forward(x, x, weight_ref, 0, vec_ref, pixels)[0]
    first_ref[...] = first
    second_ref[...] = level_forward(first, first, weight_ref, 1, vec_ref, pixels)[0]


def turn_kernel(pixels, x_ref, skip_ref, weight_ref, vec_ref, out_ref):
    x = x_ref[...]
    first = level_forward(x, x, weight_ref, 0, vec_ref, pixels)[0]
    out_ref[...] = level_forward(first, skip_ref[...], weight_ref, 1, vec_ref, pixels)[0]


def states_kernel(pixels, pairs, where_ref, *refs):
    xs, refs = refs[:pairs], refs[pairs:]
    side_ref, skip_ref, weight_ref, vec_ref, states, gradients, give_ref = refs[:4] + (
        refs[4:10], refs[10:12], refs[12]
    )
    pair = where_ref[2]
    odd = where_ref[3]
    x = jnp.where(pair == 0, xs[0][...], jnp.zeros_like(xs[0]))
    for ref in xs[1:]:
        x = x + ref[...]
    rows = x.shape[0]
    s_first = jnp.where(pair == pairs - 1, side_ref[rows:], x)
    results = []
    a, *state = level_forward(x, s_first, weight_ref, 0, vec_ref, pixels)
    results.append((s_first, state))
    s_second = jnp.where(pair < pairs // 2, a, side_ref[:rows] + skip_ref[...])
    _, *state = level_forward(a, s_second, weight_ref, 1, vec_ref, pixels)
    results.append((s_second, state))
    for level in range(2):
        _, (inv_rms, unit, normed, slope) = results[level]
        inv_ref, unit_ref, slope_ref = states[3 * level : 3 * level + 3]
        inv_ref[...] = jnp.broadcast_to(inv_rms, inv_ref.shape)
        unit_ref[...] = unit
        slope_ref[...] = slope
    (s_a, (_, _, n_a, _)), (s_b, (_, _, n_b, _)) = results
    swap = odd == 1
    gradients[0][...] = jnp.where(swap, n_b, n_a)
    gradients[1][...] = jnp.where(swap, s_b, s_a)
    give_ref[:rows] = jnp.where(swap, n_a, n_b)
    give_ref[rows:] = jnp.where(swap, s_a, s_b)


def level_backward(d, states, weight_ref, level, vec_ref, pixels):
    inv_ref, unit_ref, slope_ref = states[3 * level : 3 * level + 3]
    inv_rms = inv_ref[:, :1]
    unit = unit_ref[...]
    conv_low = (d * slope_ref[...]).astype(LOW)
    first = dot_transposed(conv_low, weight_ref[level, 1])
    middle = dot_transposed(conv_low, weight_ref[level, 2])
    last = dot_transposed(conv_low, weight_ref[level, 3])
    normed_grad = middle + earlier(first, pixels) + later(last, pixels)
    scaled = normed_grad * vec_ref[level : level + 1]
    mixed_grad = d + inv_rms * (
        scaled - unit * jnp.mean(scaled * unit, axis=-1, keepdims=True)
    )
    return conv_low, normed_grad, mixed_grad, mixed_grad.astype(LOW)


def skip_back(mixed_low, weight_ref, level):
    return dot_transposed(mixed_low, weight_ref[level, 0])


def rounded(value):
    return value.astype(LOW).astype(HIGH)


def decoder_back_kernel(pixels, d_ref, *refs):
    states, (weight_ref, vec_ref, out_ref, side_ref) = refs[:6], refs[6:]
    rows = d_ref.shape[0]
    _, _, mixed_grad, mixed_low = level_backward(
        d_ref[...].astype(HIGH), states, weight_ref, 1, vec_ref, pixels
    )
    side_ref[:rows] = skip_back(mixed_low, weight_ref, 1).astype(LOW)
    _, _, mixed_grad, mixed_low = level_backward(
        rounded(mixed_grad), states, weight_ref, 0, vec_ref, pixels
    )
    out_ref[...] = mixed_low
    side_ref[rows:] = skip_back(mixed_low, weight_ref, 0).astype(LOW)


def turn_back_kernel(pixels, d_ref, *refs):
    states, (weight_ref, vec_ref, out_ref, side_ref) = refs[:6], refs[6:]
    _, _, mixed_grad, mixed_low = level_backward(
        d_ref[...].astype(HIGH), states, weight_ref, 1, vec_ref, pixels
    )
    side_ref[...] = skip_back(mixed_low, weight_ref, 1).astype(LOW)
    _, _, mixed_grad, mixed_low = level_backward(
        rounded(mixed_grad), states, weight_ref, 0, vec_ref, pixels
    )
    out_ref[...] = (mixed_grad + skip_back(mixed_low, weight_ref, 0)).astype(LOW)


def encoder_back_kernel(pixels, d_ref, extra_ref, *refs):
    states, (weight_ref, vec_ref, out_ref) = refs[:6], refs[6:]
    _, _, mixed_grad, mixed_low = level_backward(
        d_ref[...].astype(HIGH), states, weight_ref, 1, vec_ref, pixels
    )
    d = rounded(mixed_grad + skip_back(mixed_low, weight_ref, 1)) + extra_ref[...].astype(HIGH)
    _, _, mixed_grad, mixed_low = level_backward(d, states, weight_ref, 0, vec_ref, pixels)
    out_ref[...] = (mixed_grad + skip_back(mixed_low, weight_ref, 0)).astype(LOW)


def last_kernel(pixels, pairs, where_ref, *refs):
    ds, refs = refs[:pairs], refs[pairs:]
    side_ref, extra_ref, *refs = refs
    states, (weight_ref, vec_ref, own_ref, give_ref) = refs[:6], refs[6:]
    pair = where_ref[2]
    swap = where_ref[3] == 1
    rows = extra_ref.shape[0]
    d = jnp.where(pair == pairs - 1, ds[0][...], jnp.zeros_like(ds[0])).astype(HIGH)
    for ref in ds[1:]:
        d = d + ref[...].astype(HIGH)
    d = d + side_ref[rows:].astype(HIGH)
    dc_b, normed_grad, mixed_grad, du_b = level_backward(d, states, weight_ref, 1, vec_ref, pixels)
    gain_b = jnp.sum(normed_grad * states[4][...], axis=0, keepdims=True)
    joined = mixed_grad + skip_back(du_b, weight_ref, 1)
    d = rounded(jnp.where(pair < pairs // 2, joined, mixed_grad))
    d = d + side_ref[:rows].astype(HIGH) + extra_ref[...].astype(HIGH)
    dc_a, normed_grad, mixed_grad, du_a = level_backward(d, states, weight_ref, 0, vec_ref, pixels)
    gain_a = jnp.sum(normed_grad * states[1][...], axis=0, keepdims=True)

    def put(ref, first, dc0, dc1, du0, du1, gain0, gain1):
        ref[:rows] = jnp.where(first, dc0, dc1)
        ref[rows : 2 * rows] = jnp.where(first, du0, du1)
        gain = jnp.where(first, gain0, gain1)
        high = jnp.broadcast_to(gain.astype(LOW), (GAIN_ROWS, gain.shape[1]))
        low = jnp.broadcast_to((gain - rounded(gain)).astype(LOW), high.shape)
        line = lax.broadcasted_iota(jnp.int32, high.shape, 0)
        ref[2 * rows :] = jnp.where(line == 0, high.astype(HIGH), low.astype(HIGH)).astype(LOW)

    put(own_ref, swap, dc_b, dc_a, du_b, du_a, gain_b, gain_a)
    put(give_ref, swap, dc_a, dc_b, du_a, du_b, gain_a, gain_b)


def weight_kernel(pixels, where_ref, own_ref, got_ref, n_ref, s_ref, early_ref, keep_ref, give_ref, grad_ref):
    ring, chunk, width = keep_ref.shape
    used = chunk - CHUNK_PAD
    rows = n_ref.shape[0]
    normed = jnp.concatenate([n_ref[...], early_ref[:rows]], axis=0)
    s = jnp.concatenate([s_ref[...], early_ref[rows:]], axis=0)
    mixed_low = jnp.concatenate([own_ref[rows : 2 * rows], got_ref[rows : 2 * rows]], axis=0)
    parts = [own_ref[:rows].astype(HIGH), got_ref[:rows].astype(HIGH)]
    shifted = [
        jnp.concatenate([earlier(p, pixels) for p in parts], axis=0).astype(LOW),
        jnp.concatenate(parts, axis=0).astype(LOW),
        jnp.concatenate([later(p, pixels) for p in parts], axis=0).astype(LOW),
    ]
    gain = jnp.zeros((1, width), HIGH)
    for ref in (own_ref, got_ref):
        tail = ref[2 * rows :].astype(HIGH)
        gain = gain + tail[:1] + tail[1:2]
    grad_ref[:, used:, :] = jnp.zeros((2 * ring, CHUNK_PAD, width), LOW)
    grad_ref[0, used:, :] = jnp.broadcast_to(gain, (CHUNK_PAD, width)).astype(LOW)
    each = width // used

    def put(matrix, value):
        grad_ref[matrix * each : (matrix + 1) * each, :used, :] = value.astype(LOW).reshape(
            each, used, width
        )

    put(0, dot_outer(s, mixed_low))
    for tap in range(3):
        put(tap + 1, dot_outer(normed, shifted[tap]))
    core = where_ref[0]
    z = where_ref[1]

    def share(k, carry):
        target = lax.rem(z + k, ring)
        keep_ref[k] = grad_ref[core * ring + target]
        give_ref[k] = grad_ref[(1 - core) * ring + target]
        return carry

    lax.fori_loop(0, ring, share, 0)


def gather_kernel(where_ref, *refs):
    pieces = refs[: 4 * PIECES]
    skip_ref, conv_ref, out_ref = refs[4 * PIECES :]
    odd = where_ref[3]
    place = where_ref[4]
    out_ref[odd, 0] = skip_ref[0]
    width = skip_ref.shape[1]
    for tap in range(3):
        out_ref[odd, tap + 1] = conv_ref[0, tap * width : (tap + 1) * width]
    size = width // PIECES
    for m in range(4):
        matrix = place ^ m
        for n in range(PIECES):
            out_ref[1 - odd, matrix, n * size : (n + 1) * size, :] = pieces[m * PIECES + n][...]


def finish_kernel(scale, ring, where_ref, *refs):
    own, other, (skip_ref, conv_ref, gain_ref, all_ref) = refs[:ring], refs[ring : 2 * ring], refs[2 * ring :]
    chunk, width = own[0].shape
    used = chunk - CHUNK_PAD
    core = where_ref[0]
    z = where_ref[1]
    for k in range(ring):
        target = lax.rem(z + k, ring)
        all_ref[core * ring + target] = own[k][...]
        all_ref[(1 - core) * ring + target] = other[k][...]
    each = width // used

    def place(target_ref, first):
        def step(c, carry):
            start = pl.multiple_of(c * used, used)
            target_ref[0, pl.ds(start, used), :] = all_ref[first + c, :used, :].astype(HIGH) * scale
            return carry

        return step

    lax.fori_loop(0, each, place(skip_ref, 0), 0)
    lax.fori_loop(0, 3 * each, place(conv_ref, each), 0)
    gain_ref[...] = all_ref[0, used : used + 1, :].astype(HIGH) * scale


def call(kernel, name, outs, *args, scratch=(), scalars=0, limit=SMALL_BYTES):
    specs = [pl.BlockSpec(memory_space=pltpu.SMEM)] * scalars + [
        pl.BlockSpec(memory_space=pltpu.VMEM)
    ] * (len(args) - scalars)
    return pl.pallas_call(
        kernel,
        out_shape=outs,
        in_specs=specs,
        name=name,
        scratch_shapes=scratch,
        compiler_params=pltpu.CompilerParams(vmem_limit_bytes=limit),
    )(*args)


def after(value, other):
    return lax.optimization_barrier((value, other))[0]


def make_local(sizes):
    sections = sizes["section"]
    dp = sizes["dp"]
    pairs = sections // 2
    cross = 2
    ring = dp // 4

    def local(clips, cotangent, timesteps, time_table, skip_weights, conv_weights, gains):
        both = ("section", "dp")
        section = lax.axis_index("section")
        member = lax.axis_index("dp")
        odd = section % 2
        where = jnp.stack([member % 2, member // 4, section // 2, odd, member % 4]).astype(jnp.int32)
        count, frames, pixels, width = clips.shape
        rows = frames * pixels
        low = lambda *shape: jax.ShapeDtypeStruct(shape, LOW)
        high = lambda *shape: jax.ShapeDtypeStruct(shape, HIGH)

        def move(value, section_of, member_of, only=range(sections)):
            return lax.ppermute(
                value,
                both,
                [(s * dp + i, section_of(s) * dp + member_of(i)) for s in only for i in range(dp)],
            )

        same = lambda i: i
        to_core = lambda i: i ^ 1
        to_x = lambda i: i ^ cross
        partner = lambda s: s ^ 1

        def hop(value, source, target):
            return move(
                value, lambda s: s + 2 * (target - source), same, (2 * source, 2 * source + 1)
            )

        place = member % 4
        wanted = place ^ cross
        taps = conv_weights.reshape(3, width, width)
        tap = lax.dynamic_index_in_dim(taps, jnp.maximum(wanted - 1, 0), 0, keepdims=False)
        quarter = jnp.where(wanted == 0, skip_weights[0], tap)
        size = width // PIECES
        pieces = [[None] * PIECES for _ in range(4)]
        for n in range(PIECES):
            pieces[0][n] = move(quarter[n * size : (n + 1) * size], partner, to_x)
            pieces[2][n] = move(pieces[0][n], same, to_x)
        for n in range(PIECES):
            pieces[1][n] = move(pieces[0][n], same, to_core)
        for n in range(PIECES):
            pieces[3][n] = move(pieces[2][n], same, to_core)
        embeds = jnp.take(time_table[0], timesteps, axis=0).astype(HIGH)
        is_odd = odd == 1
        mine = jnp.where(is_odd, embeds[1:2], embeds[0:1])
        theirs = jnp.where(is_odd, embeds[0:1], embeds[1:2])
        got = move(jnp.concatenate([gains, theirs], axis=0), partner, same)
        vec = jnp.concatenate(
            [
                jnp.where(is_odd, got[:1], gains),
                jnp.where(is_odd, gains, got[:1]),
                jnp.where(is_odd, got[1:2], mine),
                jnp.where(is_odd, mine, got[1:2]),
            ],
            axis=0,
        )
        weights = call(
            gather_kernel, "gather", low(2, 4, width, width),
            where, *[p for m in pieces for p in m], skip_weights, conv_weights,
            scalars=1, limit=SMALL_BYTES,
        )
        clip = jnp.where(is_odd, clips[1].reshape(rows, width), clips[0].reshape(rows, width))
        cotan = jnp.where(
            is_odd, cotangent[1].reshape(rows, width), cotangent[0].reshape(rows, width)
        )

        one = low(rows, width)
        two = low(2 * rows, width)
        bind = lambda kernel: lambda *r: kernel(pixels, *r)
        a0, a1 = call(bind(encoder_kernel), "fwd0", (one, one), clip, weights, vec)
        x1 = hop(a1, 0, 1)
        a2, a3 = call(bind(encoder_kernel), "fwd1", (one, one), x1, weights, vec)
        x2 = hop(a3, 1, 2)
        skip = hop(a2, 1, 2)
        side = hop(after(jnp.concatenate([a0, a1], axis=0), a3), 0, pairs - 1)
        a5 = call(bind(turn_kernel), "fwd2", one, x2, skip, weights, vec)
        x3 = hop(a5, 2, 3)
        state = (high(rows, 128), high(rows, width), high(rows, width))
        results = call(
            lambda *r: states_kernel(pixels, pairs, *r), "states",
            state + state + (one, one, two),
            where, clip, x1, x2, x3, side, skip, weights, vec, scalars=1,
        )
        states, (n_own, s_own, early_give) = results[:6], results[6:]

        d3, back_side = call(
            bind(decoder_back_kernel), "bwd3", (one, two), cotan, *states, weights, vec
        )
        d2 = hop(d3, 3, 2)
        g4, back_skip = call(bind(turn_back_kernel), "bwd2", (one, one), d2, *states, weights, vec)
        d1 = hop(g4, 2, 1)
        extra = hop(back_skip, 2, 1)
        sides = hop(after(back_side, g4), pairs - 1, 0)
        early = move(after(early_give, g4), partner, to_x)
        g2 = call(bind(encoder_back_kernel), "bwd1", one, d1, extra, *states, weights, vec)
        d0 = hop(g2, 1, 0)
        tall = low(2 * rows + GAIN_ROWS, width)
        own, give_late = call(
            lambda *r: last_kernel(pixels, pairs, *r), "bwd0", (tall, tall),
            where, cotan, d2, d1, d0, sides, after(extra, early), *states, weights, vec, scalars=1,
        )
        late = move(give_late, partner, to_x)

        chunk = 4 * width // (2 * ring) + CHUNK_PAD
        keep, give = call(
            bind(weight_kernel), "wgrad", (low(ring, chunk, width), low(ring, chunk, width)),
            where, own, late, n_own, s_own, early,
            scratch=[pltpu.VMEM((2 * ring, chunk, width), LOW)], scalars=1, limit=BIG_BYTES,
        )
        down = lambda i: ((i // 4 - 1) % ring) * 4 + i % 4
        up = lambda i: ((i // 4 + 1) % ring) * 4 + i % 4
        met = move(give, same, to_core)

        def total_of(k):
            return keep[k].astype(HIGH) + met[k].astype(HIGH)

        far = ring // 2
        lower = move(total_of(far).astype(LOW), same, down)
        upper = move(total_of(far - 1).astype(LOW), same, up)
        for k in range(1, far):
            lower = move((lower.astype(HIGH) + total_of(far + k)).astype(LOW), same, down)
            if k < far - 1:
                upper = move((upper.astype(HIGH) + total_of(far - 1 - k)).astype(LOW), same, up)
        part = (total_of(0) + lower.astype(HIGH) + upper.astype(HIGH)).astype(LOW)
        part = part + move(part, same, to_x)
        full = [None] * ring
        full[0] = lower = upper = part
        order = [0]
        for k in range(1, far + 1):
            full[k] = lower = move(lower, same, down)
            order.append(k)
            if k < far:
                full[ring - k] = upper = move(upper, same, up)
                order.append(ring - k)
        other = [None] * ring
        for n, k in enumerate(order):
            value = full[k]
            if n > 1:
                value = after(value, other[order[n - 2]])
            other[k] = move(value, same, to_core)
        return call(
            lambda *r: finish_kernel(1.0 / (count * dp), ring, *r), "finish",
            (high(1, width, width), high(1, 3 * width, width), high(1, width)),
            where, *full, *other,
            scratch=[pltpu.VMEM((2 * ring, chunk, width), LOW)], scalars=1, limit=BIG_BYTES,
        )

    return local


def solution(mesh):
    placed = (
        P("dp", None, None, None),
        P("dp", None, None, None),
        P("dp"),
        P("section", None, None),
        P("section", None, None),
        P("section", None, None),
        P("section", None),
    )
    return jax.shard_map(
        make_local(dict(mesh.shape)),
        mesh=mesh,
        in_specs=placed,
        out_specs=(P("section", None, None), P("section", None, None), P("section", None)),
        check_vma=False,
    )
```

```python
import jax
import jax.numpy as jnp
from jax import lax
from jax.experimental import pallas as pl
from jax.experimental.pallas import tpu as pltpu
from jax.sharding import PartitionSpec as P

EPSILON = 1e-05
LOW = jnp.bfloat16
HIGH = jnp.float32
SMALL_BYTES = 12 * 2**20
BIG_BYTES = 32 * 2**20
CHUNK_PAD = 8
GAIN_ROWS = 16
PIECES = 2


def dot(left, right):
    return lax.dot_general(left, right, (((1,), (0,)), ((), ())), preferred_element_type=HIGH)


def dot_transposed(left, right):
    return lax.dot_general(left, right, (((1,), (1,)), ((), ())), preferred_element_type=HIGH)


def dot_outer(left, right):
    return lax.dot_general(left, right, (((0,), (0,)), ((), ())), preferred_element_type=HIGH)


def later(value, pixels):
    return jnp.concatenate([jnp.zeros_like(value[:pixels]), value[:-pixels]], axis=0)


def earlier(value, pixels):
    return jnp.concatenate([value[pixels:], jnp.zeros_like(value[:pixels])], axis=0)


def level_forward(x, s, weight_ref, level, vec_ref, pixels):
    gain = vec_ref[pl.ds(level, 1), :]
    embed = vec_ref[pl.ds(2 + level, 1), :]
    mixed = x.astype(HIGH) + dot(s, weight_ref[level, 0]) + embed
    inv_rms = lax.rsqrt(jnp.mean(mixed * mixed, axis=-1, keepdims=True) + EPSILON)
    unit = mixed * inv_rms
    normed = (unit * gain).astype(LOW)
    before = dot(normed, weight_ref[level, 1])
    middle = dot(normed, weight_ref[level, 2])
    after_tap = dot(normed, weight_ref[level, 3])
    conv_out = middle + later(before, pixels) + earlier(after_tap, pixels)
    sigmoid = jax.nn.sigmoid(conv_out)
    out = (mixed + conv_out * sigmoid).astype(LOW)
    return out, inv_rms, unit, normed, sigmoid * (1.0 + conv_out * (1.0 - sigmoid))


def encoder_kernel(pixels, x_ref, weight_ref, vec_ref, first_ref, second_ref):
    def step(level, carry):
        x = second_ref[...]
        first_ref[...] = x
        second_ref[...] = level_forward(x, x, weight_ref, level, vec_ref, pixels)[0]
        return carry

    second_ref[...] = x_ref[...]
    lax.fori_loop(0, 2, step, 0)


def turn_kernel(pixels, x_ref, skip_ref, weight_ref, vec_ref, out_ref):
    def step(level, carry):
        x = out_ref[...]
        s = jnp.where(level == 0, x, skip_ref[...])
        out_ref[...] = level_forward(x, s, weight_ref, level, vec_ref, pixels)[0]
        return carry

    out_ref[...] = x_ref[...]
    lax.fori_loop(0, 2, step, 0)


def states_kernel(pixels, pairs, where_ref, *refs):
    xs, refs = refs[:pairs], refs[pairs:]
    side_ref, skip_ref, weight_ref, vec_ref = refs[:4]
    inv_ref, unit_ref, slope_ref, own_ref, give_ref, x_ref = refs[4:]
    pair = where_ref[2]
    odd = where_ref[3]
    x = jnp.where(pair == 0, xs[0][...], jnp.zeros_like(xs[0]))
    for ref in xs[1:]:
        x = x + ref[...]
    rows = x.shape[0]
    x_ref[...] = x

    def step(level, carry):
        x = x_ref[...]
        direct = jnp.logical_or(
            pair < pairs // 2, jnp.logical_and(level == 0, pair < pairs - 1)
        )
        first = jnp.where(level == 0, side_ref[rows:], side_ref[:rows] + skip_ref[...])
        s = jnp.where(direct, x, first)
        out, inv_rms, unit, normed, slope = level_forward(x, s, weight_ref, level, vec_ref, pixels)
        x_ref[...] = out
        inv_ref[level] = jnp.broadcast_to(inv_rms, inv_ref.shape[1:])
        unit_ref[level] = unit
        slope_ref[level] = slope

        def put(ref):
            ref[:rows] = normed
            ref[rows:] = s

        pl.when(level == odd)(lambda: put(own_ref))
        pl.when(level != odd)(lambda: put(give_ref))
        return carry

    lax.fori_loop(0, 2, step, 0)


def level_backward(d, states, weight_ref, level, vec_ref, pixels):
    inv_ref, unit_ref, slope_ref = states
    inv_rms = inv_ref[level][:, :1]
    unit = unit_ref[level]
    conv_low = (d * slope_ref[level]).astype(LOW)
    first = dot_transposed(conv_low, weight_ref[level, 1])
    middle = dot_transposed(conv_low, weight_ref[level, 2])
    last = dot_transposed(conv_low, weight_ref[level, 3])
    normed_grad = middle + earlier(first, pixels) + later(last, pixels)
    scaled = normed_grad * vec_ref[pl.ds(level, 1), :]
    mixed_grad = d + inv_rms * (
        scaled - unit * jnp.mean(scaled * unit, axis=-1, keepdims=True)
    )
    return conv_low, normed_grad, mixed_grad, mixed_grad.astype(LOW)


def skip_back(mixed_low, weight_ref, level):
    return dot_transposed(mixed_low, weight_ref[level, 0])


def rounded(value):
    return value.astype(LOW).astype(HIGH)


def decoder_back_kernel(pixels, d_ref, *refs):
    states, (weight_ref, vec_ref, out_ref, side_ref) = refs[:3], refs[3:]
    out_ref[...] = d_ref[...]

    def step(i, carry):
        level = 1 - i
        _, _, _, mixed_low = level_backward(
            out_ref[...].astype(HIGH), states, weight_ref, level, vec_ref, pixels
        )
        out_ref[...] = mixed_low
        side_ref[i] = skip_back(mixed_low, weight_ref, level).astype(LOW)
        return carry

    lax.fori_loop(0, 2, step, 0)


def turn_back_kernel(pixels, d_ref, *refs):
    states, (weight_ref, vec_ref, out_ref, side_ref) = refs[:3], refs[3:]
    out_ref[...] = d_ref[...]

    def step(i, carry):
        level = 1 - i
        _, _, mixed_grad, mixed_low = level_backward(
            out_ref[...].astype(HIGH), states, weight_ref, level, vec_ref, pixels
        )
        skip_grad = skip_back(mixed_low, weight_ref, level)

        @pl.when(i == 0)
        def _():
            out_ref[...] = mixed_low
            side_ref[...] = skip_grad.astype(LOW)

        @pl.when(i == 1)
        def _():
            out_ref[...] = (mixed_grad + skip_grad).astype(LOW)

        return carry

    lax.fori_loop(0, 2, step, 0)


def encoder_back_kernel(pixels, d_ref, extra_ref, *refs):
    states, (weight_ref, vec_ref, out_ref) = refs[:3], refs[3:]
    out_ref[...] = d_ref[...]

    def step(i, carry):
        level = 1 - i
        d = out_ref[...].astype(HIGH)
        d = jnp.where(i == 1, d + extra_ref[...].astype(HIGH), d)
        _, _, mixed_grad, mixed_low = level_backward(d, states, weight_ref, level, vec_ref, pixels)
        out_ref[...] = (mixed_grad + skip_back(mixed_low, weight_ref, level)).astype(LOW)
        return carry

    lax.fori_loop(0, 2, step, 0)


def last_kernel(pixels, pairs, where_ref, *refs):
    ds, refs = refs[:pairs], refs[pairs:]
    side_ref, extra_ref, *refs = refs
    states, (weight_ref, vec_ref, own_ref, give_ref, d_ref) = refs[:3], refs[3:]
    pair = where_ref[2]
    odd = where_ref[3]
    rows = extra_ref.shape[0]
    d = jnp.where(pair == pairs - 1, ds[0][...], jnp.zeros_like(ds[0])).astype(HIGH)
    for ref in ds[1:]:
        d = d + ref[...].astype(HIGH)
    d_ref[...] = d + side_ref[1].astype(HIGH)

    def step(i, carry):
        level = 1 - i
        conv_low, normed_grad, mixed_grad, mixed_low = level_backward(
            d_ref[...], states, weight_ref, level, vec_ref, pixels
        )
        gain = jnp.sum(normed_grad * states[1][level], axis=0, keepdims=True)

        @pl.when(i == 0)
        def _():
            joined = mixed_grad + skip_back(mixed_low, weight_ref, level)
            back = rounded(jnp.where(pair < pairs // 2, joined, mixed_grad))
            d_ref[...] = back + side_ref[0].astype(HIGH) + extra_ref[...].astype(HIGH)

        def put(ref):
            ref[:rows] = conv_low
            ref[rows : 2 * rows] = mixed_low
            high = jnp.broadcast_to(gain.astype(LOW), (GAIN_ROWS, gain.shape[1]))
            low = jnp.broadcast_to((gain - rounded(gain)).astype(LOW), high.shape)
            line = lax.broadcasted_iota(jnp.int32, high.shape, 0)
            ref[2 * rows :] = jnp.where(line == 0, high.astype(HIGH), low.astype(HIGH)).astype(LOW)

        pl.when(level == odd)(lambda: put(own_ref))
        pl.when(level != odd)(lambda: put(give_ref))
        return carry

    lax.fori_loop(0, 2, step, 0)


def weight_kernel(pixels, ring, where_ref, own_ref, got_ref, first_ref, early_ref, keep_ref, give_ref, grad_ref, left_ref, right_ref):
    _, chunk, width = keep_ref.shape
    used = chunk - CHUNK_PAD
    rows = first_ref.shape[0] // 2
    for n, (saved_ref, ref) in enumerate(((first_ref, own_ref), (early_ref, got_ref))):
        here = slice(n * rows, (n + 1) * rows)
        left_ref[0, here] = saved_ref[rows:]
        left_ref[1, here] = saved_ref[:rows]
        conv_grad = ref[:rows].astype(HIGH)
        right_ref[0, here] = ref[rows : 2 * rows]
        right_ref[1, here] = earlier(conv_grad, pixels).astype(LOW)
        right_ref[2, here] = ref[:rows]
        right_ref[3, here] = later(conv_grad, pixels).astype(LOW)
    gain = jnp.zeros((1, width), HIGH)
    for ref in (own_ref, got_ref):
        tail = ref[2 * rows :].astype(HIGH)
        gain = gain + tail[:1] + tail[1:2]
    grad_ref[:, used:, :] = jnp.zeros((2 * ring, CHUNK_PAD, width), LOW)
    grad_ref[0, used:, :] = jnp.broadcast_to(gain, (CHUNK_PAD, width)).astype(LOW)

    def multiply(matrix, carry):
        value = dot_outer(left_ref[jnp.minimum(matrix, 1)], right_ref[matrix]).astype(LOW)
        each = width // used
        grad_ref[pl.ds(matrix * each, each), :used, :] = value.reshape(each, used, width)
        return carry

    lax.fori_loop(0, 4, multiply, 0)
    core = where_ref[0]
    z = where_ref[1]
    side = where_ref[5]
    steps = ring // 2
    for half in range(2):
        first = (side ^ half) * ring
        for n in range(steps):
            lower = first + lax.rem(z + steps + n, ring)
            upper = first + lax.rem(z + steps - 1 - n, ring)
            keep_ref[half * steps + n] = grad_ref[jnp.where(core == 0, lower, upper)]
            give_ref[half * steps + n] = grad_ref[jnp.where(core == 0, upper, lower)]


def gather_kernel(where_ref, *refs):
    pieces = refs[: 4 * PIECES]
    skip_ref, conv_ref, out_ref = refs[4 * PIECES :]
    odd = where_ref[3]
    place = where_ref[4]
    out_ref[odd, 0] = skip_ref[0]
    width = skip_ref.shape[1]
    for tap in range(3):
        out_ref[odd, tap + 1] = conv_ref[0, tap * width : (tap + 1) * width]
    size = width // PIECES
    for m in range(4):
        matrix = place ^ m
        for n in range(PIECES):
            out_ref[1 - odd, matrix, n * size : (n + 1) * size, :] = pieces[m * PIECES + n][...]


def finish_kernel(scale, ring, where_ref, *refs):
    skip_ref, conv_ref, gain_ref, all_ref = refs[-4:]
    steps = ring // 2
    own, crossed, beside = refs[:steps], refs[steps : 2 * steps], refs[2 * steps : -4]
    chunk, width = own[0].shape
    used = chunk - CHUNK_PAD
    core = where_ref[0]
    z = where_ref[1]
    side = where_ref[5]
    other = [(ref, 2 * n) for ref in beside for n in range(ref.shape[0] // 2)]
    for n in range(steps):
        lower = lax.rem(z + 1 + n, ring)
        upper = lax.rem(z + ring - 1 - n, ring) if n < steps - 1 else z
        here = jnp.where(core == 0, lower, upper)
        there = jnp.where(core == 0, upper, lower)
        ref, at = other[n]
        all_ref[side * ring + here] = own[n][...]
        all_ref[(1 - side) * ring + here] = crossed[n][...]
        all_ref[side * ring + there] = ref[at]
        all_ref[(1 - side) * ring + there] = ref[at + 1]
    each = width // used

    def place(target_ref, first):
        def step(c, carry):
            start = pl.multiple_of(c * used, used)
            target_ref[0, pl.ds(start, used), :] = all_ref[first + c, :used, :].astype(HIGH) * scale
            return carry

        return step

    lax.fori_loop(0, each, place(skip_ref, 0), 0)
    lax.fori_loop(0, 3 * each, place(conv_ref, each), 0)
    gain_ref[...] = all_ref[0, used : used + 1, :].astype(HIGH) * scale


def call(kernel, outs, *args, scratch=(), scalars=0, limit=SMALL_BYTES):
    specs = [pl.BlockSpec(memory_space=pltpu.SMEM)] * scalars + [
        pl.BlockSpec(memory_space=pltpu.VMEM)
    ] * (len(args) - scalars)
    return pl.pallas_call(
        kernel,
        out_shape=outs,
        in_specs=specs,
        scratch_shapes=scratch,
        compiler_params=pltpu.CompilerParams(vmem_limit_bytes=limit),
    )(*args)


def after(value, other):
    return lax.optimization_barrier((value, other))[0]


def make_local(sizes):
    sections = sizes["section"]
    dp = sizes["dp"]
    pairs = sections // 2
    cross = 2
    ring = dp // 4

    def local(clips, cotangent, timesteps, time_table, skip_weights, conv_weights, gains):
        both = ("section", "dp")
        section = lax.axis_index("section")
        member = lax.axis_index("dp")
        odd = section % 2
        where = jnp.stack(
            [member % 2, member // 4, section // 2, odd, member % 4, member // 2 % 2]
        ).astype(jnp.int32)
        count, frames, pixels, width = clips.shape
        rows = frames * pixels
        low = lambda *shape: jax.ShapeDtypeStruct(shape, LOW)
        high = lambda *shape: jax.ShapeDtypeStruct(shape, HIGH)

        def move(value, section_of, member_of, only=range(sections)):
            return lax.ppermute(
                value,
                both,
                [(s * dp + i, section_of(s) * dp + member_of(i)) for s in only for i in range(dp)],
            )

        same = lambda i: i
        to_core = lambda i: i ^ 1
        to_x = lambda i: i ^ cross
        partner = lambda s: s ^ 1

        def hop(value, source, target):
            return move(
                value, lambda s: s + 2 * (target - source), same, (2 * source, 2 * source + 1)
            )

        place = member % 4
        wanted = place ^ cross
        taps = conv_weights.reshape(3, width, width)
        tap = lax.dynamic_index_in_dim(taps, jnp.maximum(wanted - 1, 0), 0, keepdims=False)
        quarter = jnp.where(wanted == 0, skip_weights[0], tap)
        size = width // PIECES
        pieces = [[None] * PIECES for _ in range(4)]
        for n in range(PIECES):
            pieces[0][n] = move(quarter[n * size : (n + 1) * size], partner, to_x)
            pieces[2][n] = move(pieces[0][n], same, to_x)
        for n in range(PIECES):
            pieces[1][n] = move(pieces[0][n], same, to_core)
        for n in range(PIECES):
            pieces[3][n] = move(pieces[2][n], same, to_core)
        embeds = jnp.take(time_table[0], timesteps, axis=0).astype(HIGH)
        is_odd = odd == 1
        mine = jnp.where(is_odd, embeds[1:2], embeds[0:1])
        theirs = jnp.where(is_odd, embeds[0:1], embeds[1:2])
        got = move(jnp.concatenate([gains, theirs], axis=0), partner, same)
        vec = jnp.concatenate(
            [
                jnp.where(is_odd, got[:1], gains),
                jnp.where(is_odd, gains, got[:1]),
                jnp.where(is_odd, got[1:2], mine),
                jnp.where(is_odd, mine, got[1:2]),
            ],
            axis=0,
        )
        weights = call(
            gather_kernel, low(2, 4, width, width),
            where, *[p for m in pieces for p in m], skip_weights, conv_weights,
            scalars=1, limit=SMALL_BYTES,
        )
        clip = jnp.where(is_odd, clips[1].reshape(rows, width), clips[0].reshape(rows, width))
        cotan = jnp.where(
            is_odd, cotangent[1].reshape(rows, width), cotangent[0].reshape(rows, width)
        )

        one = low(rows, width)
        two = low(2 * rows, width)
        bind = lambda kernel: lambda *r: kernel(pixels, *r)
        a0, a1 = call(bind(encoder_kernel), (one, one), clip, weights, vec)
        x1 = hop(a1, 0, 1)
        a2, a3 = call(bind(encoder_kernel), (one, one), x1, weights, vec)
        x2 = hop(a3, 1, 2)
        skip = hop(a2, 1, 2)
        side = hop(after(jnp.concatenate([a0, a1], axis=0), a3), 0, pairs - 1)
        a5 = call(bind(turn_kernel), one, x2, skip, weights, vec)
        x3 = hop(a5, 2, 3)
        results = call(
            lambda *r: states_kernel(pixels, pairs, *r),
            (high(2, rows, 128), high(2, rows, width), high(2, rows, width), two, two),
            where, clip, x1, x2, x3, side, skip, weights, vec, scalars=1,
            scratch=[pltpu.VMEM((rows, width), LOW)],
        )
        states, (first_own, early_give) = results[:3], results[3:]

        d3, back_side = call(
            bind(decoder_back_kernel), (one, low(2, rows, width)), cotan, *states, weights, vec
        )
        d2 = hop(d3, 3, 2)
        g4, back_skip = call(bind(turn_back_kernel), (one, one), d2, *states, weights, vec)
        d1 = hop(g4, 2, 1)
        extra = hop(back_skip, 2, 1)
        sides = hop(after(back_side, g4), pairs - 1, 0)
        early = move(after(early_give, g4), partner, to_x)
        g2 = call(bind(encoder_back_kernel), one, d1, extra, *states, weights, vec)
        d0 = hop(g2, 1, 0)
        tall = low(2 * rows + GAIN_ROWS, width)
        own, give_late = call(
            lambda *r: last_kernel(pixels, pairs, *r), (tall, tall),
            where, cotan, d2, d1, d0, sides, after(extra, early), *states, weights, vec, scalars=1,
            scratch=[pltpu.VMEM((rows, width), HIGH)],
        )
        late = move(give_late, partner, to_x)

        chunk = 2 * width // ring + CHUNK_PAD
        steps = ring // 2
        parts = low(2 * steps, chunk, width)
        keep, give = call(
            lambda *r: weight_kernel(pixels, ring, *r), (parts, parts),
            where, own, late, first_own, early,
            scratch=[
                pltpu.VMEM((2 * ring, chunk, width), LOW),
                pltpu.VMEM((2, 2 * rows, width), LOW),
                pltpu.VMEM((4, 2 * rows, width), LOW),
            ],
            scalars=1, limit=BIG_BYTES,
        )

        def turn(i):
            ahead = -1 if i % 2 == 0 else 1
            return ((i // 4 + ahead) % ring) * 4 + i % 4

        def some(value, member_of, cores=(0, 1)):
            return lax.ppermute(
                value,
                both,
                [
                    (s * dp + i, s * dp + member_of(i))
                    for s in range(sections)
                    for i in range(dp)
                    if i % 2 in cores
                ],
            )

        first_core = member % 2 == 0
        met = some(give, to_core)
        crossed = [
            some((keep[steps + n].astype(HIGH) + met[steps + n].astype(HIGH)).astype(LOW), to_x)
            for n in range(steps)
        ]

        def item(n):
            return keep[n].astype(HIGH) + met[n].astype(HIGH) + crossed[n].astype(HIGH)

        partial = item(0).astype(LOW)
        for n in range(1, steps):
            partial = (some(partial, turn).astype(HIGH) + item(n)).astype(LOW)
        partial = jnp.where(first_core, some(partial, turn, (0,)), partial)
        part = partial + some(partial, to_core)

        mine_here = []
        across = []
        value = part
        part_across = some(part, to_x, (1,))
        for _ in range(steps - 1):
            value = some(value, turn)
            mine_here.append(value)
            across.append(some(value, to_x))
        value = some(value, turn, (0,))
        mine_here.append(jnp.where(first_core, value, part))
        last_across = some(value, to_x, (0,))
        across.append(jnp.where(first_core, last_across, part_across))
        beside = []
        for span in ((0, 1), (2,), (3,)):
            stacked = jnp.stack([v for n in span for v in (mine_here[n], across[n])])
            beside.append(some(stacked, to_core))
        return call(
            lambda *r: finish_kernel(1.0 / (count * dp), ring, *r),
            (high(1, width, width), high(1, 3 * width, width), high(1, width)),
            where, *mine_here, *across, *beside,
            scratch=[pltpu.VMEM((2 * ring, chunk, width), LOW)], scalars=1, limit=BIG_BYTES,
        )

    return local


def solution(mesh):
    placed = (
        P("dp", None, None, None),
        P("dp", None, None, None),
        P("dp"),
        P("section", None, None),
        P("section", None, None),
        P("section", None, None),
        P("section", None),
    )
    return jax.shard_map(
        make_local(dict(mesh.shape)),
        mesh=mesh,
        in_specs=placed,
        out_specs=(P("section", None, None), P("section", None, None), P("section", None)),
        check_vma=False,
    )
```

```python
import jax
import jax.numpy as jnp
from jax import lax
from jax.experimental import pallas as pl
from jax.experimental.pallas import tpu as pltpu
from jax.sharding import PartitionSpec as P

EPSILON = 1e-05
LOW = jnp.bfloat16
HIGH = jnp.float32
SMALL_BYTES = 12 * 2**20
BIG_BYTES = 32 * 2**20
CHUNK_PAD = 8
GAIN_ROWS = 16
PIECES = 3
BESIDE = ((0, 3), (3, 5))


def dot(left, right):
    return lax.dot_general(left, right, (((1,), (0,)), ((), ())), preferred_element_type=HIGH)


def dot_transposed(left, right):
    return lax.dot_general(left, right, (((1,), (1,)), ((), ())), preferred_element_type=HIGH)


def dot_outer(left, right):
    return lax.dot_general(left, right, (((0,), (0,)), ((), ())), preferred_element_type=HIGH)


def later(value, pixels):
    return jnp.concatenate([jnp.zeros_like(value[:pixels]), value[:-pixels]], axis=0)


def earlier(value, pixels):
    return jnp.concatenate([value[pixels:], jnp.zeros_like(value[:pixels])], axis=0)


def level_forward(x, s, weight_ref, level, vec_ref, pixels):
    gain = vec_ref[pl.ds(level, 1), :]
    embed = vec_ref[pl.ds(2 + level, 1), :]
    mixed = x.astype(HIGH) + dot(s, weight_ref[level, 0]) + embed
    inv_rms = lax.rsqrt(jnp.mean(mixed * mixed, axis=-1, keepdims=True) + EPSILON)
    unit = mixed * inv_rms
    normed = (unit * gain).astype(LOW)
    before = dot(normed, weight_ref[level, 1])
    middle = dot(normed, weight_ref[level, 2])
    after_tap = dot(normed, weight_ref[level, 3])
    conv_out = middle + later(before, pixels) + earlier(after_tap, pixels)
    sigmoid = jax.nn.sigmoid(conv_out)
    out = (mixed + conv_out * sigmoid).astype(LOW)
    return out, inv_rms, unit, normed, sigmoid * (1.0 + conv_out * (1.0 - sigmoid))


def encoder_kernel(pixels, x_ref, weight_ref, vec_ref, first_ref, second_ref):
    def step(level, carry):
        x = second_ref[...]
        first_ref[...] = x
        second_ref[...] = level_forward(x, x, weight_ref, level, vec_ref, pixels)[0]
        return carry

    second_ref[...] = x_ref[...]
    lax.fori_loop(0, 2, step, 0)


def turn_kernel(pixels, x_ref, skip_ref, weight_ref, vec_ref, out_ref):
    def step(level, carry):
        x = out_ref[...]
        s = jnp.where(level == 0, x, skip_ref[...])
        out_ref[...] = level_forward(x, s, weight_ref, level, vec_ref, pixels)[0]
        return carry

    out_ref[...] = x_ref[...]
    lax.fori_loop(0, 2, step, 0)


def states_kernel(pixels, pairs, where_ref, *refs):
    xs, refs = refs[:pairs], refs[pairs:]
    side_ref, skip_ref, weight_ref, vec_ref = refs[:4]
    inv_ref, unit_ref, slope_ref, own_ref, give_ref, x_ref = refs[4:]
    pair = where_ref[2]
    odd = where_ref[3]
    x = jnp.where(pair == 0, xs[0][...], jnp.zeros_like(xs[0]))
    for ref in xs[1:]:
        x = x + ref[...]
    rows = x.shape[0]
    x_ref[...] = x

    def step(level, carry):
        x = x_ref[...]
        direct = jnp.logical_or(
            pair < pairs // 2, jnp.logical_and(level == 0, pair < pairs - 1)
        )
        first = jnp.where(level == 0, side_ref[rows:], side_ref[:rows] + skip_ref[...])
        s = jnp.where(direct, x, first)
        out, inv_rms, unit, normed, slope = level_forward(x, s, weight_ref, level, vec_ref, pixels)
        x_ref[...] = out
        inv_ref[level] = jnp.broadcast_to(inv_rms, inv_ref.shape[1:])
        unit_ref[level] = unit
        slope_ref[level] = slope

        def put(ref):
            ref[:rows] = normed
            ref[rows:] = s

        pl.when(level == odd)(lambda: put(own_ref))
        pl.when(level != odd)(lambda: put(give_ref))
        return carry

    lax.fori_loop(0, 2, step, 0)


def level_backward(d, states, weight_ref, level, vec_ref, pixels):
    inv_ref, unit_ref, slope_ref = states
    inv_rms = inv_ref[level][:, :1]
    unit = unit_ref[level]
    conv_low = (d * slope_ref[level]).astype(LOW)
    first = dot_transposed(conv_low, weight_ref[level, 1])
    middle = dot_transposed(conv_low, weight_ref[level, 2])
    last = dot_transposed(conv_low, weight_ref[level, 3])
    normed_grad = middle + earlier(first, pixels) + later(last, pixels)
    scaled = normed_grad * vec_ref[pl.ds(level, 1), :]
    mixed_grad = d + inv_rms * (
        scaled - unit * jnp.mean(scaled * unit, axis=-1, keepdims=True)
    )
    return conv_low, normed_grad, mixed_grad, mixed_grad.astype(LOW)


def skip_back(mixed_low, weight_ref, level):
    return dot_transposed(mixed_low, weight_ref[level, 0])


def rounded(value):
    return value.astype(LOW).astype(HIGH)


def decoder_back_kernel(pixels, d_ref, *refs):
    states, (weight_ref, vec_ref, out_ref, side_ref) = refs[:3], refs[3:]
    out_ref[...] = d_ref[...]

    def step(i, carry):
        level = 1 - i
        _, _, _, mixed_low = level_backward(
            out_ref[...].astype(HIGH), states, weight_ref, level, vec_ref, pixels
        )
        out_ref[...] = mixed_low
        side_ref[i] = skip_back(mixed_low, weight_ref, level).astype(LOW)
        return carry

    lax.fori_loop(0, 2, step, 0)


def turn_back_kernel(pixels, d_ref, *refs):
    states, (weight_ref, vec_ref, out_ref, side_ref) = refs[:3], refs[3:]
    out_ref[...] = d_ref[...]

    def step(i, carry):
        level = 1 - i
        _, _, mixed_grad, mixed_low = level_backward(
            out_ref[...].astype(HIGH), states, weight_ref, level, vec_ref, pixels
        )
        skip_grad = skip_back(mixed_low, weight_ref, level)

        @pl.when(i == 0)
        def _():
            out_ref[...] = mixed_low
            side_ref[...] = skip_grad.astype(LOW)

        @pl.when(i == 1)
        def _():
            out_ref[...] = (mixed_grad + skip_grad).astype(LOW)

        return carry

    lax.fori_loop(0, 2, step, 0)


def encoder_back_kernel(pixels, d_ref, extra_ref, *refs):
    states, (weight_ref, vec_ref, out_ref) = refs[:3], refs[3:]
    out_ref[...] = d_ref[...]

    def step(i, carry):
        level = 1 - i
        d = out_ref[...].astype(HIGH)
        d = jnp.where(i == 1, d + extra_ref[...].astype(HIGH), d)
        _, _, mixed_grad, mixed_low = level_backward(d, states, weight_ref, level, vec_ref, pixels)
        out_ref[...] = (mixed_grad + skip_back(mixed_low, weight_ref, level)).astype(LOW)
        return carry

    lax.fori_loop(0, 2, step, 0)


def last_kernel(pixels, pairs, where_ref, *refs):
    ds, refs = refs[:pairs], refs[pairs:]
    side_ref, extra_ref, *refs = refs
    states, (weight_ref, vec_ref, own_ref, give_ref, d_ref) = refs[:3], refs[3:]
    pair = where_ref[2]
    odd = where_ref[3]
    rows = extra_ref.shape[0]
    d = jnp.where(pair == pairs - 1, ds[0][...], jnp.zeros_like(ds[0])).astype(HIGH)
    for ref in ds[1:]:
        d = d + ref[...].astype(HIGH)
    d_ref[...] = d + side_ref[1].astype(HIGH)

    def step(i, carry):
        level = 1 - i
        conv_low, normed_grad, mixed_grad, mixed_low = level_backward(
            d_ref[...], states, weight_ref, level, vec_ref, pixels
        )
        gain = jnp.sum(normed_grad * states[1][level], axis=0, keepdims=True)

        @pl.when(i == 0)
        def _():
            joined = mixed_grad + skip_back(mixed_low, weight_ref, level)
            back = rounded(jnp.where(pair < pairs // 2, joined, mixed_grad))
            d_ref[...] = back + side_ref[0].astype(HIGH) + extra_ref[...].astype(HIGH)

        def put(ref):
            ref[:rows] = conv_low
            ref[rows : 2 * rows] = mixed_low
            high = jnp.broadcast_to(gain.astype(LOW), (GAIN_ROWS, gain.shape[1]))
            low = jnp.broadcast_to((gain - rounded(gain)).astype(LOW), high.shape)
            line = lax.broadcasted_iota(jnp.int32, high.shape, 0)
            ref[2 * rows :] = jnp.where(line == 0, high.astype(HIGH), low.astype(HIGH)).astype(LOW)

        pl.when(level == odd)(lambda: put(own_ref))
        pl.when(level != odd)(lambda: put(give_ref))
        return carry

    lax.fori_loop(0, 2, step, 0)


def weight_kernel(pixels, ring, where_ref, own_ref, got_ref, first_ref, early_ref, keep_ref, give_ref, grad_ref, left_ref, right_ref):
    _, chunk, width = keep_ref.shape
    used = chunk - CHUNK_PAD
    rows = first_ref.shape[0] // 2
    for n, (saved_ref, ref) in enumerate(((first_ref, own_ref), (early_ref, got_ref))):
        here = slice(n * rows, (n + 1) * rows)
        left_ref[0, here] = saved_ref[rows:]
        left_ref[1, here] = saved_ref[:rows]
        conv_grad = ref[:rows].astype(HIGH)
        right_ref[0, here] = ref[rows : 2 * rows]
        right_ref[1, here] = earlier(conv_grad, pixels).astype(LOW)
        right_ref[2, here] = ref[:rows]
        right_ref[3, here] = later(conv_grad, pixels).astype(LOW)
    gain = jnp.zeros((1, width), HIGH)
    for ref in (own_ref, got_ref):
        tail = ref[2 * rows :].astype(HIGH)
        gain = gain + tail[:1] + tail[1:2]
    grad_ref[:, used:, :] = jnp.zeros((4 * ring, CHUNK_PAD, width), LOW)
    grad_ref[0, used:, :] = jnp.broadcast_to(gain, (CHUNK_PAD, width)).astype(LOW)

    def multiply(matrix, carry):
        value = dot_outer(left_ref[jnp.minimum(matrix, 1)], right_ref[matrix]).astype(LOW)
        grad_ref[pl.ds(pl.multiple_of(matrix * ring, ring), ring), :used, :] = value.reshape(
            ring, used, width
        )
        return carry

    lax.fori_loop(0, 4, multiply, 0)
    core = where_ref[0]
    z = where_ref[1]
    side = where_ref[5]

    def share(k, carry):
        target = lax.rem(z + k, ring)
        half = side ^ (k // ring)
        keep_ref[k] = grad_ref[(core * 2 + half) * ring + target]
        give_ref[k] = grad_ref[((1 - core) * 2 + half) * ring + target]
        return carry

    lax.fori_loop(0, 2 * ring, share, 0)


def gather_kernel(spans, where_ref, *refs):
    skip_ref, conv_ref, out_ref = refs[len(spans) :]
    odd = where_ref[3]
    place = where_ref[4]
    width = skip_ref.shape[1]

    def own(tap, carry):
        start = pl.multiple_of(tap * width, width)
        out_ref[odd, tap + 1] = conv_ref[0, pl.ds(start, width), :]
        return carry

    out_ref[odd, 0] = skip_ref[0]
    lax.fori_loop(0, 3, own, 0)
    for ref, (m, start, stop) in zip(refs, spans):
        out_ref[1 - odd, place ^ m, start:stop, :] = ref[...]


def finish_kernel(scale, ring, groups, where_ref, *refs):
    skip_ref, conv_ref, gain_ref, all_ref = refs[-4:]
    chunk, _ = refs[0].shape[1:]
    used = chunk - CHUNK_PAD
    core = where_ref[0]
    z = where_ref[1]
    side = where_ref[5]
    count = len(groups)
    own, crossed, beside = refs[:count], refs[count : 2 * count], refs[2 * count : -4]
    other = []
    for ref, (first, stop) in zip(beside, BESIDE):
        at = 0
        for g in range(first, stop):
            other.append((ref, at))
            at += 2 * len(groups[g])
    for g, group in enumerate(groups):
        ref, at = other[g]
        for n, k in enumerate(group):
            target = lax.rem(z + k, ring)
            all_ref[(core * 2 + side) * ring + target] = own[g][n]
            all_ref[(core * 2 + 1 - side) * ring + target] = crossed[g][n]
            all_ref[((1 - core) * 2 + side) * ring + target] = ref[at + n]
            all_ref[((1 - core) * 2 + 1 - side) * ring + target] = ref[at + len(group) + n]

    def place(target_ref, first):
        def step(c, carry):
            start = pl.multiple_of(c * used, used)
            target_ref[0, pl.ds(start, used), :] = all_ref[first + c, :used, :].astype(HIGH) * scale
            return carry

        return step

    lax.fori_loop(0, ring, place(skip_ref, 0), 0)
    lax.fori_loop(0, 3 * ring, place(conv_ref, ring), 0)
    gain_ref[...] = all_ref[0, used : used + 1, :].astype(HIGH) * scale


def call(kernel, outs, *args, scratch=(), scalars=0, limit=SMALL_BYTES):
    specs = [pl.BlockSpec(memory_space=pltpu.SMEM)] * scalars + [
        pl.BlockSpec(memory_space=pltpu.VMEM)
    ] * (len(args) - scalars)
    return pl.pallas_call(
        kernel,
        out_shape=outs,
        in_specs=specs,
        scratch_shapes=scratch,
        compiler_params=pltpu.CompilerParams(vmem_limit_bytes=limit),
    )(*args)


def after(value, other):
    return lax.optimization_barrier((value, other))[0]


def make_local(sizes):
    sections = sizes["section"]
    dp = sizes["dp"]
    pairs = sections // 2
    cross = 2
    ring = dp // 4

    def local(clips, cotangent, timesteps, time_table, skip_weights, conv_weights, gains):
        both = ("section", "dp")
        section = lax.axis_index("section")
        member = lax.axis_index("dp")
        odd = section % 2
        where = jnp.stack(
            [member % 2, member // 4, section // 2, odd, member % 4, member // 2 % 2]
        ).astype(jnp.int32)
        count, frames, pixels, width = clips.shape
        rows = frames * pixels
        low = lambda *shape: jax.ShapeDtypeStruct(shape, LOW)
        high = lambda *shape: jax.ShapeDtypeStruct(shape, HIGH)

        def move(value, section_of, member_of, only=range(sections)):
            return lax.ppermute(
                value,
                both,
                [(s * dp + i, section_of(s) * dp + member_of(i)) for s in only for i in range(dp)],
            )

        same = lambda i: i
        to_core = lambda i: i ^ 1
        to_x = lambda i: i ^ cross
        partner = lambda s: s ^ 1

        def hop(value, source, target):
            return move(
                value, lambda s: s + 2 * (target - source), same, (2 * source, 2 * source + 1)
            )

        place = member % 4
        wanted = place ^ cross
        taps = conv_weights.reshape(3, width, width)
        tap = lax.dynamic_index_in_dim(taps, jnp.maximum(wanted - 1, 0), 0, keepdims=False)
        quarter = jnp.where(wanted == 0, skip_weights[0], tap)
        cuts = [(width * n // PIECES + 15) // 16 * 16 for n in range(PIECES + 1)]
        direct = []
        relayed = []
        for n in range(PIECES):
            piece = move(quarter[cuts[n] : cuts[n + 1]], partner, to_x)
            direct.append(piece)
            relayed.append(move(piece, same, to_x))
        spans = []
        pieces = []
        for m, part_list in ((0, direct), (2, relayed)):
            for n in range(PIECES):
                pieces.append(part_list[n])
                spans.append((m, cuts[n], cuts[n + 1]))
        pieces += [
            move(jnp.concatenate(direct, axis=0), same, to_core),
            move(jnp.concatenate(relayed[:-1], axis=0), same, to_core),
            move(relayed[-1], same, to_core),
        ]
        spans += [(1, 0, width), (3, 0, cuts[-2]), (3, cuts[-2], width)]
        embeds = jnp.take(time_table[0], timesteps, axis=0).astype(HIGH)
        is_odd = odd == 1
        mine = jnp.where(is_odd, embeds[1:2], embeds[0:1])
        theirs = jnp.where(is_odd, embeds[0:1], embeds[1:2])
        got = move(jnp.concatenate([gains, theirs], axis=0), partner, same)
        vec = jnp.concatenate(
            [
                jnp.where(is_odd, got[:1], gains),
                jnp.where(is_odd, gains, got[:1]),
                jnp.where(is_odd, got[1:2], mine),
                jnp.where(is_odd, mine, got[1:2]),
            ],
            axis=0,
        )
        weights = call(
            lambda *r: gather_kernel(spans, *r), low(2, 4, width, width),
            where, *pieces, skip_weights, conv_weights,
            scalars=1, limit=SMALL_BYTES,
        )
        clip = jnp.where(is_odd, clips[1].reshape(rows, width), clips[0].reshape(rows, width))
        cotan = jnp.where(
            is_odd, cotangent[1].reshape(rows, width), cotangent[0].reshape(rows, width)
        )

        one = low(rows, width)
        two = low(2 * rows, width)
        bind = lambda kernel: lambda *r: kernel(pixels, *r)
        a0, a1 = call(bind(encoder_kernel), (one, one), clip, weights, vec)
        x1 = hop(a1, 0, 1)
        a2, a3 = call(bind(encoder_kernel), (one, one), x1, weights, vec)
        x2 = hop(a3, 1, 2)
        skip = hop(a2, 1, 2)
        side = hop(after(jnp.concatenate([a0, a1], axis=0), a3), 0, pairs - 1)
        a5 = call(bind(turn_kernel), one, x2, skip, weights, vec)
        x3 = hop(a5, 2, 3)
        results = call(
            lambda *r: states_kernel(pixels, pairs, *r),
            (high(2, rows, 128), high(2, rows, width), high(2, rows, width), two, two),
            where, clip, x1, x2, x3, side, skip, weights, vec, scalars=1,
            scratch=[pltpu.VMEM((rows, width), LOW)],
        )
        states, (first_own, early_give) = results[:3], results[3:]

        d3, back_side = call(
            bind(decoder_back_kernel), (one, low(2, rows, width)), cotan, *states, weights, vec
        )
        d2 = hop(d3, 3, 2)
        g4, back_skip = call(bind(turn_back_kernel), (one, one), d2, *states, weights, vec)
        d1 = hop(g4, 2, 1)
        extra = hop(back_skip, 2, 1)
        sides = hop(after(back_side, g4), pairs - 1, 0)
        early = move(after(early_give, g4), partner, to_x)
        g2 = call(bind(encoder_back_kernel), one, d1, extra, *states, weights, vec)
        d0 = hop(g2, 1, 0)
        tall = low(2 * rows + GAIN_ROWS, width)
        own, give_late = call(
            lambda *r: last_kernel(pixels, pairs, *r), (tall, tall),
            where, cotan, d2, d1, d0, sides, after(extra, early), *states, weights, vec, scalars=1,
            scratch=[pltpu.VMEM((rows, width), HIGH)],
        )
        late = move(give_late, partner, to_x)

        chunk = width // ring + CHUNK_PAD
        parts = low(2 * ring, chunk, width)
        keep, give = call(
            lambda *r: weight_kernel(pixels, ring, *r), (parts, parts),
            where, own, late, first_own, early,
            scratch=[
                pltpu.VMEM((4 * ring, chunk, width), LOW),
                pltpu.VMEM((2, 2 * rows, width), LOW),
                pltpu.VMEM((4, 2 * rows, width), LOW),
            ],
            scalars=1, limit=BIG_BYTES,
        )
        down = lambda i: ((i // 4 - 1) % ring) * 4 + i % 4
        up = lambda i: ((i // 4 + 1) % ring) * 4 + i % 4
        met = move(give, same, to_core)
        far = ring // 2
        waves = [(far + n, far - 1 - n) for n in range(far)]
        crossed = {}
        for wave in waves:
            out = jnp.stack(
                [(keep[ring + k].astype(HIGH) + met[ring + k].astype(HIGH)).astype(LOW) for k in wave]
            )
            back = move(out, same, to_x)
            for n, k in enumerate(wave):
                crossed[k] = back[n]

        def total_of(k):
            return keep[k].astype(HIGH) + met[k].astype(HIGH) + crossed[k].astype(HIGH)

        lower = move(total_of(far).astype(LOW), same, down)
        upper = move(total_of(far - 1).astype(LOW), same, up)
        for k in range(1, far):
            lower = move((lower.astype(HIGH) + total_of(far + k)).astype(LOW), same, down)
            if k < far - 1:
                upper = move((upper.astype(HIGH) + total_of(far - 1 - k)).astype(LOW), same, up)
        part = (total_of(0) + lower.astype(HIGH) + upper.astype(HIGH)).astype(LOW)
        groups = [(0,)] + [(k, ring - k) for k in range(1, far)] + [(far,)]
        lower = upper = part
        mine_here = [part[None]]
        across = [move(mine_here[0], same, to_x)]
        for group in groups[1:]:
            if len(group) > 1:
                upper = move(upper, same, up)
            lower = move(lower, same, down)
            mine_here.append(jnp.stack([lower, upper][: len(group)]))
            across.append(move(mine_here[-1], same, to_x))
        beside = []
        for first, stop in BESIDE:
            stacked = [v for n in range(first, stop) for v in (mine_here[n], across[n])]
            beside.append(move(jnp.concatenate(stacked, axis=0), same, to_core))
        gathered = mine_here + across + beside
        return call(
            lambda *r: finish_kernel(1.0 / (count * dp), ring, groups, *r),
            (high(1, width, width), high(1, 3 * width, width), high(1, width)),
            where, *gathered,
            scratch=[pltpu.VMEM((4 * ring, chunk, width), LOW)], scalars=1, limit=BIG_BYTES,
        )

    return local


def solution(mesh):
    placed = (
        P("dp", None, None, None),
        P("dp", None, None, None),
        P("dp"),
        P("section", None, None),
        P("section", None, None),
        P("section", None, None),
        P("section", None),
    )
    return jax.shard_map(
        make_local(dict(mesh.shape)),
        mesh=mesh,
        in_specs=placed,
        out_specs=(P("section", None, None), P("section", None, None), P("section", None)),
        check_vma=False,
    )
```

```python
import jax
import jax.numpy as jnp
from jax import lax
from jax.experimental import pallas as pl
from jax.experimental.pallas import tpu as pltpu
from jax.sharding import PartitionSpec as P

EPSILON = 1e-05
LOW = jnp.bfloat16
HIGH = jnp.float32
SMALL_BYTES = 12 * 2**20
BIG_BYTES = 32 * 2**20
CHUNK_PAD = 8
GAIN_ROWS = 16
PIECES = 3
BESIDE = ((0, 3), (3, 5))


def dot(left, right):
    return lax.dot_general(left, right, (((1,), (0,)), ((), ())), preferred_element_type=HIGH)


def dot_transposed(left, right):
    return lax.dot_general(left, right, (((1,), (1,)), ((), ())), preferred_element_type=HIGH)


def dot_outer(left, right):
    return lax.dot_general(left, right, (((0,), (0,)), ((), ())), preferred_element_type=HIGH)


def later(value, pixels):
    return jnp.concatenate([jnp.zeros_like(value[:pixels]), value[:-pixels]], axis=0)


def earlier(value, pixels):
    return jnp.concatenate([value[pixels:], jnp.zeros_like(value[:pixels])], axis=0)


def level_forward(x, s, weight_ref, level, vec_ref, pixels):
    gain = vec_ref[pl.ds(level, 1), :]
    embed = vec_ref[pl.ds(2 + level, 1), :]
    mixed = x.astype(HIGH) + dot(s, weight_ref[level, 0]) + embed
    inv_rms = lax.rsqrt(jnp.mean(mixed * mixed, axis=-1, keepdims=True) + EPSILON)
    unit = mixed * inv_rms
    normed = (unit * gain).astype(LOW)
    before = dot(normed, weight_ref[level, 1])
    middle = dot(normed, weight_ref[level, 2])
    after_tap = dot(normed, weight_ref[level, 3])
    conv_out = middle + later(before, pixels) + earlier(after_tap, pixels)
    sigmoid = jax.nn.sigmoid(conv_out)
    out = (mixed + conv_out * sigmoid).astype(LOW)
    return out, inv_rms, unit, normed, sigmoid * (1.0 + conv_out * (1.0 - sigmoid))


def encoder_kernel(pixels, x_ref, weight_ref, vec_ref, first_ref, second_ref):
    def step(level, carry):
        x = second_ref[...]
        first_ref[...] = x
        second_ref[...] = level_forward(x, x, weight_ref, level, vec_ref, pixels)[0]
        return carry

    second_ref[...] = x_ref[...]
    lax.fori_loop(0, 2, step, 0)


def turn_kernel(pixels, x_ref, skip_ref, weight_ref, vec_ref, out_ref):
    def step(level, carry):
        x = out_ref[...]
        s = jnp.where(level == 0, x, skip_ref[...])
        out_ref[...] = level_forward(x, s, weight_ref, level, vec_ref, pixels)[0]
        return carry

    out_ref[...] = x_ref[...]
    lax.fori_loop(0, 2, step, 0)


def states_kernel(pixels, pairs, where_ref, *refs):
    xs, refs = refs[:pairs], refs[pairs:]
    side_ref, skip_ref, weight_ref, vec_ref = refs[:4]
    inv_ref, unit_ref, slope_ref, own_ref, give_ref, x_ref = refs[4:]
    pair = where_ref[2]
    odd = where_ref[3]
    x = jnp.where(pair == 0, xs[0][...], jnp.zeros_like(xs[0]))
    for ref in xs[1:]:
        x = x + ref[...]
    rows = x.shape[0]
    x_ref[...] = x

    def step(level, carry):
        x = x_ref[...]
        direct = jnp.logical_or(
            pair < pairs // 2, jnp.logical_and(level == 0, pair < pairs - 1)
        )
        first = jnp.where(level == 0, side_ref[rows:], side_ref[:rows] + skip_ref[...])
        s = jnp.where(direct, x, first)
        out, inv_rms, unit, normed, slope = level_forward(x, s, weight_ref, level, vec_ref, pixels)
        x_ref[...] = out
        inv_ref[level] = jnp.broadcast_to(inv_rms, inv_ref.shape[1:])
        unit_ref[level] = unit
        slope_ref[level] = slope

        def put(ref):
            ref[:rows] = normed
            ref[rows:] = s

        pl.when(level == odd)(lambda: put(own_ref))
        pl.when(level != odd)(lambda: put(give_ref))
        return carry

    lax.fori_loop(0, 2, step, 0)


def level_backward(d, states, weight_ref, level, vec_ref, pixels):
    inv_ref, unit_ref, slope_ref = states
    inv_rms = inv_ref[level][:, :1]
    unit = unit_ref[level]
    conv_low = (d * slope_ref[level]).astype(LOW)
    first = dot_transposed(conv_low, weight_ref[level, 1])
    middle = dot_transposed(conv_low, weight_ref[level, 2])
    last = dot_transposed(conv_low, weight_ref[level, 3])
    normed_grad = middle + earlier(first, pixels) + later(last, pixels)
    scaled = normed_grad * vec_ref[pl.ds(level, 1), :]
    mixed_grad = d + inv_rms * (
        scaled - unit * jnp.mean(scaled * unit, axis=-1, keepdims=True)
    )
    return conv_low, normed_grad, mixed_grad, mixed_grad.astype(LOW)


def skip_back(mixed_low, weight_ref, level):
    return dot_transposed(mixed_low, weight_ref[level, 0])


def rounded(value):
    return value.astype(LOW).astype(HIGH)


def decoder_back_kernel(pixels, d_ref, *refs):
    states, (weight_ref, vec_ref, out_ref, side_ref) = refs[:3], refs[3:]
    out_ref[...] = d_ref[...]

    def step(i, carry):
        level = 1 - i
        _, _, _, mixed_low = level_backward(
            out_ref[...].astype(HIGH), states, weight_ref, level, vec_ref, pixels
        )
        out_ref[...] = mixed_low
        side_ref[i] = skip_back(mixed_low, weight_ref, level).astype(LOW)
        return carry

    lax.fori_loop(0, 2, step, 0)


def turn_back_kernel(pixels, d_ref, *refs):
    states, (weight_ref, vec_ref, out_ref, side_ref) = refs[:3], refs[3:]
    out_ref[...] = d_ref[...]

    def step(i, carry):
        level = 1 - i
        _, _, mixed_grad, mixed_low = level_backward(
            out_ref[...].astype(HIGH), states, weight_ref, level, vec_ref, pixels
        )
        skip_grad = skip_back(mixed_low, weight_ref, level)

        @pl.when(i == 0)
        def _():
            out_ref[...] = mixed_low
            side_ref[...] = skip_grad.astype(LOW)

        @pl.when(i == 1)
        def _():
            out_ref[...] = (mixed_grad + skip_grad).astype(LOW)

        return carry

    lax.fori_loop(0, 2, step, 0)


def encoder_back_kernel(pixels, d_ref, extra_ref, *refs):
    states, (weight_ref, vec_ref, out_ref) = refs[:3], refs[3:]
    out_ref[...] = d_ref[...]

    def step(i, carry):
        level = 1 - i
        d = out_ref[...].astype(HIGH)
        d = jnp.where(i == 1, d + extra_ref[...].astype(HIGH), d)
        _, _, mixed_grad, mixed_low = level_backward(d, states, weight_ref, level, vec_ref, pixels)
        out_ref[...] = (mixed_grad + skip_back(mixed_low, weight_ref, level)).astype(LOW)
        return carry

    lax.fori_loop(0, 2, step, 0)


def last_kernel(pixels, pairs, where_ref, *refs):
    ds, refs = refs[:pairs], refs[pairs:]
    side_ref, extra_ref, *refs = refs
    states, (weight_ref, vec_ref, own_ref, give_ref, d_ref) = refs[:3], refs[3:]
    pair = where_ref[2]
    odd = where_ref[3]
    rows = extra_ref.shape[0]
    d = jnp.where(pair == pairs - 1, ds[0][...], jnp.zeros_like(ds[0])).astype(HIGH)
    for ref in ds[1:]:
        d = d + ref[...].astype(HIGH)
    d_ref[...] = d + side_ref[1].astype(HIGH)

    def step(i, carry):
        level = 1 - i
        conv_low, normed_grad, mixed_grad, mixed_low = level_backward(
            d_ref[...], states, weight_ref, level, vec_ref, pixels
        )
        gain = jnp.sum(normed_grad * states[1][level], axis=0, keepdims=True)

        @pl.when(i == 0)
        def _():
            joined = mixed_grad + skip_back(mixed_low, weight_ref, level)
            back = rounded(jnp.where(pair < pairs // 2, joined, mixed_grad))
            d_ref[...] = back + side_ref[0].astype(HIGH) + extra_ref[...].astype(HIGH)

        def put(ref):
            ref[:rows] = conv_low
            ref[rows : 2 * rows] = mixed_low
            high = jnp.broadcast_to(gain.astype(LOW), (GAIN_ROWS, gain.shape[1]))
            low = jnp.broadcast_to((gain - rounded(gain)).astype(LOW), high.shape)
            line = lax.broadcasted_iota(jnp.int32, high.shape, 0)
            ref[2 * rows :] = jnp.where(line == 0, high.astype(HIGH), low.astype(HIGH)).astype(LOW)

        pl.when(level == odd)(lambda: put(own_ref))
        pl.when(level != odd)(lambda: put(give_ref))
        return carry

    lax.fori_loop(0, 2, step, 0)


def weight_kernel(pixels, ring, where_ref, own_ref, got_ref, first_ref, early_ref, keep_ref, give_ref, grad_ref, left_ref, right_ref):
    _, chunk, width = keep_ref.shape
    used = chunk - CHUNK_PAD
    rows = first_ref.shape[0] // 2
    for n, (saved_ref, ref) in enumerate(((first_ref, own_ref), (early_ref, got_ref))):
        here = slice(n * rows, (n + 1) * rows)
        left_ref[0, here] = saved_ref[rows:]
        left_ref[1, here] = saved_ref[:rows]
        conv_grad = ref[:rows].astype(HIGH)
        right_ref[0, here] = ref[rows : 2 * rows]
        right_ref[1, here] = earlier(conv_grad, pixels).astype(LOW)
        right_ref[2, here] = ref[:rows]
        right_ref[3, here] = later(conv_grad, pixels).astype(LOW)
    gain = jnp.zeros((1, width), HIGH)
    for ref in (own_ref, got_ref):
        tail = ref[2 * rows :].astype(HIGH)
        gain = gain + tail[:1] + tail[1:2]
    grad_ref[:, used:, :] = jnp.zeros((4 * ring, CHUNK_PAD, width), LOW)
    grad_ref[0, used:, :] = jnp.broadcast_to(gain, (CHUNK_PAD, width)).astype(LOW)

    def multiply(matrix, carry):
        value = dot_outer(left_ref[jnp.minimum(matrix, 1)], right_ref[matrix]).astype(LOW)
        grad_ref[pl.ds(pl.multiple_of(matrix * ring, ring), ring), :used, :] = value.reshape(
            ring, used, width
        )
        return carry

    lax.fori_loop(0, 4, multiply, 0)
    core = where_ref[0]
    z = where_ref[1]
    side = where_ref[5]

    def share(k, carry):
        target = lax.rem(z + k, ring)
        half = side ^ (k // ring)
        keep_ref[k] = grad_ref[(core * 2 + half) * ring + target]
        give_ref[k] = grad_ref[((1 - core) * 2 + half) * ring + target]
        return carry

    lax.fori_loop(0, 2 * ring, share, 0)


def own_kernel(where_ref, skip_ref, conv_ref, out_ref):
    odd = where_ref[3]
    width = skip_ref.shape[1]

    def own(tap, carry):
        start = pl.multiple_of(tap * width, width)
        out_ref[odd, tap + 1] = conv_ref[0, pl.ds(start, width), :]
        return carry

    out_ref[odd, 0] = skip_ref[0]
    lax.fori_loop(0, 3, own, 0)


def gather_kernel(spans, where_ref, *refs):
    out_ref = refs[-1]
    odd = where_ref[3]
    place = where_ref[4]
    for ref, (m, start, stop) in zip(refs, spans):
        out_ref[1 - odd, place ^ m, start:stop, :] = ref[...]


def finish_kernel(scale, ring, groups, where_ref, *refs):
    skip_ref, conv_ref, gain_ref, all_ref, wide_ref, sem_ref = refs[-6:]
    chunk, width = refs[0].shape[1:]
    used = chunk - CHUNK_PAD
    core = where_ref[0]
    z = where_ref[1]
    side = where_ref[5]
    count = len(groups)
    own, crossed, beside = refs[:count], refs[count : 2 * count], refs[2 * count : -6]
    other = []
    for ref, (first, stop) in zip(beside, BESIDE):
        at = 0
        for g in range(first, stop):
            other.append((ref, at))
            at += 2 * len(groups[g])
    for g, group in enumerate(groups):
        ref, at = other[g]
        for n, k in enumerate(group):
            target = lax.rem(z + k, ring)
            all_ref[(core * 2 + side) * ring + target] = own[g][n]
            all_ref[(core * 2 + 1 - side) * ring + target] = crossed[g][n]
            all_ref[((1 - core) * 2 + side) * ring + target] = ref[at + n]
            all_ref[((1 - core) * 2 + 1 - side) * ring + target] = ref[at + len(group) + n]

    copies = []
    for matrix in range(4):

        def step(c, carry):
            start = pl.multiple_of(c * used, used)
            value = all_ref[matrix * ring + c, :used, :].astype(HIGH) * scale
            wide_ref[matrix, pl.ds(start, used), :] = value
            return carry

        lax.fori_loop(0, ring, step, 0)
        if matrix == 0:
            target = skip_ref.at[0]
        else:
            target = conv_ref.at[0, (matrix - 1) * width : matrix * width, :]
        copies.append(pltpu.make_async_copy(wide_ref.at[matrix], target, sem_ref.at[matrix]))
        copies[-1].start()
    gain_ref[...] = all_ref[0, used : used + 1, :].astype(HIGH) * scale
    for each in copies:
        each.wait()


def call(kernel, outs, *args, scratch=(), scalars=0, limit=SMALL_BYTES, aliases=None, out_specs=None):
    specs = [pl.BlockSpec(memory_space=pltpu.SMEM)] * scalars + [
        pl.BlockSpec(memory_space=pltpu.VMEM)
    ] * (len(args) - scalars)
    return pl.pallas_call(
        kernel,
        out_shape=outs,
        in_specs=specs,
        scratch_shapes=scratch,
        input_output_aliases=aliases or {},
        **({} if out_specs is None else {"out_specs": out_specs}),
        compiler_params=pltpu.CompilerParams(vmem_limit_bytes=limit),
    )(*args)


def after(value, other):
    return lax.optimization_barrier((value, other))[0]


def make_local(sizes):
    sections = sizes["section"]
    dp = sizes["dp"]
    pairs = sections // 2
    cross = 2
    ring = dp // 4

    def local(clips, cotangent, timesteps, time_table, skip_weights, conv_weights, gains):
        both = ("section", "dp")
        section = lax.axis_index("section")
        member = lax.axis_index("dp")
        odd = section % 2
        where = jnp.stack(
            [member % 2, member // 4, section // 2, odd, member % 4, member // 2 % 2]
        ).astype(jnp.int32)
        count, frames, pixels, width = clips.shape
        rows = frames * pixels
        low = lambda *shape: jax.ShapeDtypeStruct(shape, LOW)
        high = lambda *shape: jax.ShapeDtypeStruct(shape, HIGH)

        def move(value, section_of, member_of, only=range(sections)):
            return lax.ppermute(
                value,
                both,
                [(s * dp + i, section_of(s) * dp + member_of(i)) for s in only for i in range(dp)],
            )

        same = lambda i: i
        to_core = lambda i: i ^ 1
        to_x = lambda i: i ^ cross
        partner = lambda s: s ^ 1

        def hop(value, source, target):
            return move(
                value, lambda s: s + 2 * (target - source), same, (2 * source, 2 * source + 1)
            )

        place = member % 4
        wanted = place ^ cross
        taps = conv_weights.reshape(3, width, width)
        tap = lax.dynamic_index_in_dim(taps, jnp.maximum(wanted - 1, 0), 0, keepdims=False)
        quarter = jnp.where(wanted == 0, skip_weights[0], tap)
        cuts = [(width * n // PIECES + 15) // 16 * 16 for n in range(PIECES + 1)]
        direct = []
        relayed = []
        for n in range(PIECES):
            piece = move(quarter[cuts[n] : cuts[n + 1]], partner, to_x)
            direct.append(piece)
            relayed.append(move(piece, same, to_x))
        spans = []
        pieces = []
        for m, part_list in ((0, direct), (2, relayed)):
            for n in range(PIECES):
                pieces.append(part_list[n])
                spans.append((m, cuts[n], cuts[n + 1]))
        pieces += [
            move(jnp.concatenate(direct, axis=0), same, to_core),
            move(jnp.concatenate(relayed[:-1], axis=0), same, to_core),
            move(relayed[-1], same, to_core),
        ]
        spans += [(1, 0, width), (3, 0, cuts[-2]), (3, cuts[-2], width)]
        embeds = jnp.take(time_table[0], timesteps, axis=0).astype(HIGH)
        is_odd = odd == 1
        mine = jnp.where(is_odd, embeds[1:2], embeds[0:1])
        theirs = jnp.where(is_odd, embeds[0:1], embeds[1:2])
        got = move(jnp.concatenate([gains, theirs], axis=0), partner, same)
        vec = jnp.concatenate(
            [
                jnp.where(is_odd, got[:1], gains),
                jnp.where(is_odd, gains, got[:1]),
                jnp.where(is_odd, got[1:2], mine),
                jnp.where(is_odd, mine, got[1:2]),
            ],
            axis=0,
        )
        half_weights = call(
            own_kernel, low(2, 4, width, width), where, skip_weights, conv_weights,
            scalars=1, out_specs=pl.BlockSpec(memory_space=pltpu.VMEM),
        )
        weights = call(
            lambda *r: gather_kernel(spans, *r), low(2, 4, width, width),
            where, *pieces, half_weights, aliases={1 + len(pieces): 0},
            out_specs=pl.BlockSpec(memory_space=pltpu.VMEM),
            scalars=1, limit=SMALL_BYTES,
        )
        clip = jnp.where(is_odd, clips[1].reshape(rows, width), clips[0].reshape(rows, width))
        cotan = jnp.where(
            is_odd, cotangent[1].reshape(rows, width), cotangent[0].reshape(rows, width)
        )

        one = low(rows, width)
        two = low(2 * rows, width)
        bind = lambda kernel: lambda *r: kernel(pixels, *r)
        a0, a1 = call(bind(encoder_kernel), (one, one), clip, weights, vec)
        x1 = hop(a1, 0, 1)
        a2, a3 = call(bind(encoder_kernel), (one, one), x1, weights, vec)
        x2 = hop(a3, 1, 2)
        skip = hop(a2, 1, 2)
        side = hop(after(jnp.concatenate([a0, a1], axis=0), a3), 0, pairs - 1)
        a5 = call(bind(turn_kernel), one, x2, skip, weights, vec)
        x3 = hop(a5, 2, 3)
        results = call(
            lambda *r: states_kernel(pixels, pairs, *r),
            (high(2, rows, 128), high(2, rows, width), high(2, rows, width), two, two),
            where, clip, x1, x2, x3, side, skip, weights, vec, scalars=1,
            scratch=[pltpu.VMEM((rows, width), LOW)],
        )
        states, (first_own, early_give) = results[:3], results[3:]

        d3, back_side = call(
            bind(decoder_back_kernel), (one, low(2, rows, width)), cotan, *states, weights, vec
        )
        d2 = hop(d3, 3, 2)
        g4, back_skip = call(bind(turn_back_kernel), (one, one), d2, *states, weights, vec)
        d1 = hop(g4, 2, 1)
        extra = hop(back_skip, 2, 1)
        sides = hop(after(back_side, g4), pairs - 1, 0)
        early = move(after(early_give, g4), partner, to_x)
        g2 = call(bind(encoder_back_kernel), one, d1, extra, *states, weights, vec)
        d0 = hop(g2, 1, 0)
        tall = low(2 * rows + GAIN_ROWS, width)
        own, give_late = call(
            lambda *r: last_kernel(pixels, pairs, *r), (tall, tall),
            where, cotan, d2, d1, d0, sides, after(extra, early), *states, weights, vec, scalars=1,
            scratch=[pltpu.VMEM((rows, width), HIGH)],
        )
        late = move(give_late, partner, to_x)

        chunk = width // ring + CHUNK_PAD
        parts = low(2 * ring, chunk, width)
        keep, give = call(
            lambda *r: weight_kernel(pixels, ring, *r), (parts, parts),
            where, own, late, first_own, early,
            scratch=[
                pltpu.VMEM((4 * ring, chunk, width), LOW),
                pltpu.VMEM((2, 2 * rows, width), LOW),
                pltpu.VMEM((4, 2 * rows, width), LOW),
            ],
            scalars=1, limit=BIG_BYTES,
        )
        down = lambda i: ((i // 4 - 1) % ring) * 4 + i % 4
        up = lambda i: ((i // 4 + 1) % ring) * 4 + i % 4
        met = move(give, same, to_core)
        far = ring // 2
        waves = [(far + n, far - 1 - n) for n in range(far)]
        crossed = {}
        for wave in waves:
            out = jnp.stack(
                [(keep[ring + k].astype(HIGH) + met[ring + k].astype(HIGH)).astype(LOW) for k in wave]
            )
            back = move(out, same, to_x)
            for n, k in enumerate(wave):
                crossed[k] = back[n]

        def total_of(k):
            return keep[k].astype(HIGH) + met[k].astype(HIGH) + crossed[k].astype(HIGH)

        lower = move(total_of(far).astype(LOW), same, down)
        upper = move(total_of(far - 1).astype(LOW), same, up)
        for k in range(1, far):
            lower = move((lower.astype(HIGH) + total_of(far + k)).astype(LOW), same, down)
            if k < far - 1:
                upper = move((upper.astype(HIGH) + total_of(far - 1 - k)).astype(LOW), same, up)
        part = (total_of(0) + lower.astype(HIGH) + upper.astype(HIGH)).astype(LOW)
        groups = [(0,)] + [(k, ring - k) for k in range(1, far)] + [(far,)]
        lower = upper = part
        mine_here = [part[None]]
        across = [move(mine_here[0], same, to_x)]
        for group in groups[1:]:
            if len(group) > 1:
                upper = move(upper, same, up)
            lower = move(lower, same, down)
            mine_here.append(jnp.stack([lower, upper][: len(group)]))
            across.append(move(mine_here[-1], same, to_x))
        beside = []
        for first, stop in BESIDE:
            stacked = [v for n in range(first, stop) for v in (mine_here[n], across[n])]
            beside.append(move(jnp.concatenate(stacked, axis=0), same, to_core))
        gathered = mine_here + across + beside
        return call(
            lambda *r: finish_kernel(1.0 / (count * dp), ring, groups, *r),
            (high(1, width, width), high(1, 3 * width, width), high(1, width)),
            where, *gathered,
            scratch=[
                pltpu.VMEM((4 * ring, chunk, width), LOW),
                pltpu.VMEM((4, width, width), HIGH),
                pltpu.SemaphoreType.DMA((4,)),
            ],
            scalars=1, limit=BIG_BYTES,
            out_specs=(
                pl.BlockSpec(memory_space=pl.ANY),
                pl.BlockSpec(memory_space=pl.ANY),
                pl.BlockSpec(memory_space=pltpu.VMEM),
            ),
        )

    return local


def solution(mesh):
    placed = (
        P("dp", None, None, None),
        P("dp", None, None, None),
        P("dp"),
        P("section", None, None),
        P("section", None, None),
        P("section", None, None),
        P("section", None),
    )
    return jax.shard_map(
        make_local(dict(mesh.shape)),
        mesh=mesh,
        in_specs=placed,
        out_specs=(P("section", None, None), P("section", None, None), P("section", None)),
        check_vma=False,
    )
```
